128 devices in a mesh: section: 4 (over x), expert: 32 (over z, y, core).
Axes of the slice: x: 4, y: 4, z: 4, core: 2. Of those that a mesh axis runs over, the one named last changes fastest.
Arguments:
- upstream: bfloat16 [4, 4096, 3584], P('section', 'expert'), may hold values from -0.59765625 to 0.59765625
- routes: int32 [4, 4096, 2], P('section', 'expert'), may hold values from 0 to 7, all different within a row; in each aligned block of 128 rows (0 to 127, 128 to 255, ..., all dimensions but the last counted through in order) at most 48 rows name the same one
- gates: float32 [4, 4096, 2], P('section', 'expert'), may hold values from 0.1 to 1
- w_gate: bfloat16 [4, 3584, 8192], P('section', None, 'expert'), may hold values from -0.09375 to 0.09375
- w_up: bfloat16 [4, 3584, 8192], P('section', None, 'expert'), may hold values from -0.09375 to 0.09375
- w_down: bfloat16 [4, 8192, 3584], P('section', 'expert'), may hold values from -0.1875 to 0.1875
- stash_q: bfloat16 [4, 49152, 3584], P('section', 'expert'), may hold values from -448 to 448
- stash_scale: float32 [4, 49152, 28], P('section', 'expert'), may hold values from 0.004 to 0.04
Outputs:
- grad_input: bfloat16 [4, 4096, 3584], P('section', 'expert')
- grad_gates: float32 [4, 4096, 2], P('section', 'expert')
- grad_w_gate: bfloat16 [4, 3584, 8192], P('section', None, 'expert')
- grad_w_up: bfloat16 [4, 3584, 8192], P('section', None, 'expert')
- grad_w_down: bfloat16 [4, 8192, 3584], P('section', 'expert')
The draws below stay inside these ranges and needn't reach their ends.
Inputs may be any that keep to these rules, and one draw needn't show every extreme that they name: `routes`: in each section, each token names 2 different experts, and within the 128 tokens of one device no expert is named more than 48 times; some expert is named exactly 48 times.
All inputs are finite; a program needn't handle non-finite values.
Results may differ from the reference program's by a relative error of at most 0.014.
Values may be sent and summed in bfloat16 or wider, within the bound.
A program may use at most 256 MiB of HBM per device.

```python
import math
import jax
import jax.numpy as jnp
import numpy as np
from jax import lax

D = 3584
FF = 1024
EXPERTS = 8
TOPK = 2
TOK_DEV = 128
CAP = 48
SLOTS = 1536
TOKENS = 4096
SECTIONS = 4
N_SECTION = 4
N_EXPERT = 32


def level_of(key, shape, pieces, smallest, largest):
    factor_of, own = 1.0, jax.random.fold_in(key, 6)
    for dim, blocks in pieces:
        draws = jnp.exp(jax.random.uniform(jax.random.fold_in(own, dim), (blocks,), jnp.float32, smallest / len(pieces), largest / len(pieces)))
        factor_of = factor_of * jnp.repeat(draws, shape[dim] // blocks).reshape([-1 if axis == dim else 1 for axis in range(len(shape))])
    return factor_of


def shared_out(own_key, own, number, rows, amount, top, limit, skew):
    order = jax.random.permutation(own_key, amount)
    heavy_load, common = shares(amount, rows * top, limit, skew, True), shares(amount, rows * top, limit, skew, False)
    places = jnp.arange(amount)

    def named(sizes, offset_by):
        used = int((sizes > 0).sum())
        fixed = max(1, used // 4)
        shifted = fixed + (places - fixed + offset_by * (used - fixed)) % max(1, amount - fixed)
        return jnp.zeros((amount,), jnp.int32).at[order[jnp.where(places < fixed, places, shifted)]].set(jnp.asarray(sizes, jnp.int32))

    sizes = jnp.where(number % 4 == 0, named(heavy_load, number // 4), named(common, number - number // 4 - 1))
    mixed = jax.random.permutation(jax.random.fold_in(own, 3), amount)
    donor, taker = mixed[0:amount // 2 * 2:2], mixed[1:amount // 2 * 2:2]
    slack = jnp.minimum(sizes[donor] - 1, limit - sizes[taker]) // 2
    slack = jnp.where((donor == order[0]) | (taker == order[0]) | (sizes[taker] == 0), 0, jnp.maximum(slack, 0))
    shifted = jax.random.randint(jax.random.fold_in(own, 4), (amount // 2,), 0, 1 << 20) % (slack + 1)
    sizes = sizes.at[donor].add(-shifted).at[taker].add(shifted)
    labels = jnp.searchsorted(jnp.cumsum(sizes), jnp.arange(rows * top), side="right").astype(jnp.int32)
    listing = labels.reshape(top, rows).T
    listing = listing[jax.random.permutation(jax.random.fold_in(own, 1), rows)]
    offset_by = jax.random.randint(jax.random.fold_in(own, 2), (rows, 1), 0, top)
    return jnp.take_along_axis(listing, (jnp.arange(top)[None, :] + offset_by) % top, axis=1)


def shares(count, total, limit, slope, full):
    portions = [(1 << 20) // math.isqrt(standing ** slope) + 1 for standing in range(1, count + 1)]
    largest = limit if full else min(limit, max(-(-total // count), total * portions[0] // sum(portions)))
    least = 1 if total - largest >= count - 1 else 0
    holding, rest = [largest] + [least] * (count - 1), total - largest - least * (count - 1)
    while rest > 0:
        movable = [i for i in range(1, count) if holding[i] < largest] or [i for i in range(1, count) if holding[i] < limit]
        pool, left = sum([portions[i] for i in movable]), rest
        for i in movable:
            addition = min(limit - holding[i], max(1, left * portions[i] // pool), rest)
            holding[i] = holding[i] + addition
            rest = rest - addition
    return np.array(holding)


def centred(own_key, extent, spread, limit, pieces=(), kind=jnp.bfloat16):
    values = spread * jax.random.normal(own_key, extent, jnp.float32)
    if pieces:
        values = values * level_of(own_key, extent, pieces, -0.22, 0.18)
    return jnp.clip(values, -limit, limit).astype(kind)


def setup_inputs(seed: int = 0) -> dict:
    key_list = jax.random.split(jax.random.key(seed), 9)
    upstream = centred(key_list[0], (SECTIONS, TOKENS, D), 0.1, 0.59765625, ((0, 4), (1, 32)))
    routes_keys = jax.random.split(jax.random.fold_in(key_list[1], 1), SECTIONS * TOKENS // TOK_DEV)
    routes_turns = jax.random.permutation(jax.random.fold_in(key_list[1], 3), SECTIONS * TOKENS // TOK_DEV)
    routes = jax.vmap(lambda own, number: shared_out(jax.random.fold_in(key_list[1], 2), own, number, TOK_DEV, EXPERTS, TOPK, CAP, 2))(routes_keys, routes_turns).reshape((SECTIONS, TOKENS, TOPK))
    gates = jnp.clip(jnp.exp(math.log(1.0) - 2.3025851 * jax.random.uniform(key_list[2], (SECTIONS, TOKENS, TOPK), jnp.float32) ** level_of(key_list[2], (SECTIONS, TOKENS, TOPK), ((0, 4), (1, 32)), -0.2, 0.2)), 0.1, 1.0)
    w_gate = centred(key_list[3], (SECTIONS, D, EXPERTS * FF), D ** -0.5, 0.09375, ((0, 4), (2, 32)))
    w_up = centred(key_list[4], (SECTIONS, D, EXPERTS * FF), D ** -0.5, 0.09375, ((0, 4), (2, 32)))
    w_down = centred(key_list[5], (SECTIONS, EXPERTS * FF, D), FF ** -0.5, 0.1875, ((0, 4), (1, 32)))
    stash_q = centred(key_list[6], (SECTIONS, N_EXPERT * SLOTS, D), 64.0, 448.0, ((0, 4), (1, 32)))
    stash_scale = jnp.clip(jnp.exp(math.log(0.04) - 2.30258502 * jax.random.uniform(key_list[7], (SECTIONS, N_EXPERT * SLOTS, D // 128), jnp.float32) ** level_of(key_list[7], (SECTIONS, N_EXPERT * SLOTS, D // 128), ((0, 4), (1, 32)), -0.2, 0.2)), 0.004, 0.04)
    return {"upstream": upstream, "routes": routes, "gates": gates, "w_gate": w_gate, "w_up": w_up, "w_down": w_down, "stash_q": stash_q, "stash_scale": stash_scale}


def slot_work(codes, scales, cotangent, weights, gate_cols, up_cols, down_rows):
    count, width = codes.shape
    blocks = width // 128
    inputs = (codes.astype(jnp.float32).reshape(count, blocks, 128) * scales[:, :, None]).reshape(count, width).astype(jnp.bfloat16)
    gate_pre = jnp.dot(inputs, gate_cols, preferred_element_type=jnp.float32)
    up_pre = jnp.dot(inputs, up_cols, preferred_element_type=jnp.float32)
    sigma = jax.nn.sigmoid(gate_pre)
    swish = gate_pre * sigma
    hidden = swish * up_pre
    scaled_hidden = (weights[:, None] * hidden).astype(jnp.bfloat16)
    grad_down = lax.dot_general(scaled_hidden, cotangent, (((0,), (0,)), ((), ())), preferred_element_type=jnp.float32)
    raw_grad = lax.dot_general(cotangent, down_rows, (((1,), (1,)), ((), ())), preferred_element_type=jnp.float32)
    gate_part = jnp.sum(hidden * raw_grad, axis=1)
    grad_hidden = weights[:, None] * raw_grad
    grad_gate_pre = (grad_hidden * up_pre * sigma * (1.0 + gate_pre * (1.0 - sigma))).astype(jnp.bfloat16)
    grad_up_pre = (grad_hidden * swish).astype(jnp.bfloat16)
    grad_gate_w = lax.dot_general(inputs, grad_gate_pre, (((0,), (0,)), ((), ())), preferred_element_type=jnp.float32)
    grad_up_w = lax.dot_general(inputs, grad_up_pre, (((0,), (0,)), ((), ())), preferred_element_type=jnp.float32)
    input_sum = lax.dot_general(grad_gate_pre, gate_cols, (((1,), (1,)), ((), ())), preferred_element_type=jnp.float32)
    input_sum = input_sum + lax.dot_general(grad_up_pre, up_cols, (((1,), (1,)), ((), ())), preferred_element_type=jnp.float32)
    return grad_gate_w, grad_up_w, grad_down, input_sum.astype(jnp.bfloat16), gate_part


def section_pass(cotangent, routing, gate_vals, gate_w, up_w, down_w, codes, scales):
    hsplit = N_EXPERT // EXPERTS
    ff_dev = FF // hsplit
    slots = CAP * N_EXPERT
    pairs = TOK_DEV * TOPK
    flat = routing.reshape(N_EXPERT, pairs).astype(jnp.int32)
    onehot = (flat[:, :, None] == jnp.arange(EXPERTS, dtype=jnp.int32)[None, None, :]).astype(jnp.int32)
    before = jnp.cumsum(onehot, axis=1) - onehot
    slot = jnp.sum(before * onehot, axis=2).astype(jnp.int32)
    source = jnp.arange(N_EXPERT, dtype=jnp.int32)[:, None]
    target = ((flat * N_EXPERT + source) * CAP + slot).reshape(-1).astype(jnp.int32)
    token = (jnp.arange(pairs, dtype=jnp.int32)[None, :] // TOPK + source * TOK_DEV).reshape(-1).astype(jnp.int32)
    row_buf = jnp.zeros((EXPERTS * slots, D), jnp.bfloat16).at[target].set(cotangent[token])
    weight_buf = jnp.zeros((EXPERTS * slots,), jnp.float32).at[target].set(gate_vals.reshape(-1))
    row_buf = row_buf.reshape(EXPERTS, slots, D)
    weight_buf = weight_buf.reshape(EXPERTS, slots)

    def device(index):
        expert = index // hsplit
        rows = lax.dynamic_index_in_dim(row_buf, expert, 0, keepdims=False)
        weights = lax.dynamic_index_in_dim(weight_buf, expert, 0, keepdims=False)
        gate_cols = lax.dynamic_slice_in_dim(gate_w, index * ff_dev, ff_dev, 1)
        up_cols = lax.dynamic_slice_in_dim(up_w, index * ff_dev, ff_dev, 1)
        down_rows = lax.dynamic_slice_in_dim(down_w, index * ff_dev, ff_dev, 0)
        code_rows = lax.dynamic_slice_in_dim(codes, index * slots, slots, 0)
        scale_rows = lax.dynamic_slice_in_dim(scales, index * slots, slots, 0)
        return slot_work(code_rows, scale_rows, rows, weights, gate_cols, up_cols, down_rows)

    grad_gw, grad_uw, grad_dw, input_part, gate_part = lax.map(device, jnp.arange(N_EXPERT, dtype=jnp.int32))
    summed = jnp.sum(input_part.reshape(EXPERTS, hsplit, slots, D).astype(jnp.float32), axis=1).reshape(EXPERTS * slots, D)
    gate_sum = jnp.sum(gate_part.reshape(EXPERTS, hsplit, slots), axis=1).reshape(EXPERTS * slots)
    grad_input = jnp.sum(summed[target].reshape(N_EXPERT * TOK_DEV, TOPK, D), axis=1).astype(jnp.bfloat16)
    grad_gates = gate_sum[target].reshape(N_EXPERT * TOK_DEV, TOPK)
    grad_gw = jnp.transpose(grad_gw, (1, 0, 2)).reshape(D, N_EXPERT * ff_dev).astype(jnp.bfloat16)
    grad_uw = jnp.transpose(grad_uw, (1, 0, 2)).reshape(D, N_EXPERT * ff_dev).astype(jnp.bfloat16)
    grad_dw = grad_dw.reshape(N_EXPERT * ff_dev, D).astype(jnp.bfloat16)
    return grad_input, grad_gates, grad_gw, grad_uw, grad_dw


def reference(upstream, routes, gates, w_gate, w_up, w_down, stash_q, stash_scale):
    results = []
    for section_index in range(N_SECTION):
        nxt = (section_index + 1) % N_SECTION
        results.append(section_pass(upstream[nxt], routes[section_index], gates[section_index], w_gate[section_index], w_up[section_index], w_down[section_index], stash_q[section_index], stash_scale[section_index]))
    return (jnp.stack([item[0] for item in results]), jnp.stack([item[1] for item in results]), jnp.stack([item[2] for item in results]), jnp.stack([item[3] for item in results]), jnp.stack([item[4] for item in results]))
```

```python
import functools

import jax
import jax.numpy as jnp
from jax import lax
from jax.experimental import pallas as pl
from jax.experimental.pallas import tpu as pltpu
from jax.sharding import PartitionSpec as P

EXPERTS = 8
CAP = 48
NCHIP = 16
NDEV = 32
CH = 256
D = 3584
HALF = D // 2
NK = HALF // CH
SLOTS = NDEV * CAP
FD = 256
TOK = 128
FR = 256
NFR = SLOTS // FR
QR = 64
MESH = pl.DeviceIdType.MESH
BF = jnp.bfloat16
F32 = jnp.float32


def dot(a, b, ca, cb):
    return lax.dot_general(a, b, (((ca,), (cb,)), ((), ())), preferred_element_type=F32)


def wait_bytes(ref, sem):
    pltpu.make_async_copy(ref, ref, sem).wait()


def kernel(
    nsec,
    routes, gates, up, wg_h, wu_h, wd_h, sq_h, ss_h,
    gi_h, gg_o, gwg_h, gwu_h, gwd_h,
    rows, inputs, wg, wu, wd, ga, gb, hid, raw, sh, dg, du,
    send, xbuf, comb, psend, back, gout, gsib, scale, gmat, tgt,
    gsend, grecv, gpsend, gprecv, st_d, st_g, st_u,
    x_send, x_recv, d_send, d_recv, s_send, s_recv, p_send, p_recv,
    c_send, c_recv, gm_send, gm_recv, g_send, g_recv, gp_send, gp_recv,
    gi_send, gi_recv, w_sem, sq_sem, ss_sem, o_sem, go_sem,
):
    sec = lax.axis_index("section")
    me = lax.axis_index("expert")
    chip = me // 2
    core = me % 2
    sib = me + 1 - 2 * core
    other = 1 - core
    down = (sec + nsec - 1) % nsec
    upper = (sec + 1) % nsec

    pltpu.make_async_copy(ss_h, scale, ss_sem).start()
    for r in range(NFR):
        pltpu.make_async_copy(
            sq_h.at[pl.ds(r * FR, FR)], inputs.at[pl.ds(r * FR, FR)], sq_sem.at[r]
        ).start()
    pltpu.make_async_copy(wg_h, wg, w_sem.at[0]).start()
    pltpu.make_async_copy(wu_h, wu, w_sem.at[1]).start()
    for j in range(2 * NK):
        pltpu.make_async_copy(wd_h.at[:, pl.ds(j * CH, CH)], wd.at[j], w_sem.at[2 + j]).start()

    bar = pltpu.get_barrier_semaphore()

    def greet(o, _):
        pl.semaphore_signal(
            bar, inc=1, device_id=(sec, (me + o) % NDEV), device_id_type=MESH
        )
        return 0

    lax.fori_loop(1, NDEV, greet, 0)
    for sx in (down, upper):
        for cc in range(2):
            pl.semaphore_signal(
                bar, inc=1, device_id=(sx, chip * 2 + cc), device_id_type=MESH
            )
    pl.semaphore_wait(bar, NDEV - 1 + 4)

    def xs(k, _):
        for cc in range(2):
            pltpu.make_async_remote_copy(
                src_ref=up.at[:, pl.ds(pl.multiple_of(cc * HALF + k * CH, CH), CH)],
                dst_ref=xbuf.at[k, core],
                send_sem=x_send,
                recv_sem=x_recv.at[k],
                device_id=(down, chip * 2 + cc),
                device_id_type=MESH,
            ).start()
        return 0

    lax.fori_loop(0, NK, xs, 0)

    lane = lax.broadcasted_iota(jnp.int32, (TOK, TOK), 1)
    sub = lax.broadcasted_iota(jnp.int32, (TOK, TOK), 0)
    r0 = routes[:, 0:1]
    r1 = routes[:, 1:2]
    o0 = (lane == r0).astype(F32)
    o1 = (lane == r1).astype(F32)
    lower = (lane < sub).astype(BF)
    before = dot(lower, (o0 + o1).astype(BF), 1, 0)
    t0 = r0 * CAP + jnp.sum(before * o0, axis=1, keepdims=True).astype(jnp.int32)
    t1 = r1 * CAP + jnp.sum(before * o1, axis=1, keepdims=True).astype(jnp.int32)
    tgt[0] = jnp.broadcast_to(t0, (TOK, TOK))
    tgt[1] = jnp.broadcast_to(t1, (TOK, TOK))
    wide = lax.broadcasted_iota(jnp.int32, (TOK, EXPERTS * CAP), 1)
    gmat[core] = ((wide == t0) | (wide == t1)).astype(F32).astype(BF)
    for e in range(EXPERTS):
        at = lane + e * CAP
        inside = lane < CAP
        hit = jnp.where((at == t0) & inside, gates[:, 0:1], 0.0) + jnp.where(
            (at == t1) & inside, gates[:, 1:2], 0.0
        )
        gsend[e] = jnp.broadcast_to(jnp.sum(hit, axis=0, keepdims=True), (8, TOK))
    pltpu.make_async_remote_copy(
        src_ref=gmat.at[core], dst_ref=gmat.at[core], send_sem=gm_send, recv_sem=gm_recv,
        device_id=(sec, sib), device_id_type=MESH,
    ).start()

    def sendg(o, _):
        to = (me + o) % NDEV
        pltpu.make_async_remote_copy(
            src_ref=gsend.at[to // 4], dst_ref=grecv.at[me], send_sem=g_send,
            recv_sem=g_recv, device_id=(sec, to), device_id_type=MESH,
        ).start()
        return 0

    lax.fori_loop(1, NDEV, sendg, 0)
    pltpu.make_async_copy(gsend.at[me // 4], grecv.at[me], g_recv).start()
    wait_bytes(gmat.at[0], gm_recv)

    pltpu.make_async_copy(ss_h, scale, ss_sem).wait()
    pltpu.make_async_copy(wg_h, wg, w_sem.at[0]).wait()
    pltpu.make_async_copy(wu_h, wu, w_sem.at[1]).wait()

    def dispatch(k, _):
        wait_bytes(xbuf.at[k], x_recv.at[k])
        for b in range(2):
            packed = dot(gmat[b], xbuf[k, b], 0, 0).astype(BF)
            send[k, :, b] = packed.reshape(EXPERTS, CAP, CH)

        def out(o, _):
            to = (chip + o) % NCHIP
            pltpu.make_async_remote_copy(
                src_ref=send.at[k, to // 2],
                dst_ref=rows.at[core * NK + k, pl.ds(chip * 2, 2)],
                send_sem=d_send.at[k], recv_sem=d_recv.at[k],
                device_id=(sec, to * 2 + core), device_id_type=MESH,
            ).start()
            return 0

        lax.fori_loop(1, NCHIP, out, 0)
        pltpu.make_async_copy(
            send.at[k, chip // 2], rows.at[core * NK + k, pl.ds(chip * 2, 2)], d_recv.at[k]
        ).start()

        @pl.when(k < NFR)
        def _():
            base = pl.multiple_of(k * FR, FR)
            wait_bytes(inputs.at[pl.ds(base, FR)], sq_sem.at[k])

            def dequant(q, _):
                at = pl.multiple_of(base + q * QR, QR)
                sc = scale[pl.ds(at, QR), :]
                for n in range(D // 128):
                    cols = slice(n * 128, (n + 1) * 128)
                    v = inputs[pl.ds(at, QR), cols].astype(F32) * sc[:, n : n + 1]
                    inputs[pl.ds(at, QR), cols] = v.astype(BF)
                return 0

            lax.fori_loop(0, FR // QR, dequant, 0)
            ga[pl.ds(base, FR)] = dot(inputs[pl.ds(base, FR)], wg[...], 1, 0)
            gb[pl.ds(base, FR)] = dot(inputs[pl.ds(base, FR)], wu[...], 1, 0)

        return 0

    lax.fori_loop(0, NK, dispatch, 0)

    wait_bytes(grecv, g_recv)
    diag = lax.broadcasted_iota(jnp.int32, (CAP, TOK), 0) == lax.broadcasted_iota(
        jnp.int32, (CAP, TOK), 1
    )

    def factors(b, _):
        at = pl.ds(pl.multiple_of(b * CAP, CAP), CAP)
        w = jnp.sum(jnp.where(diag, grecv[b][0:1], 0.0), axis=1, keepdims=True)
        g = ga[at]
        u = gb[at]
        sigma = jax.nn.sigmoid(g)
        swish = g * sigma
        h = swish * u
        hid[at] = h
        sh[at] = (w * h).astype(BF)
        ga[at] = w * u * sigma * (1.0 + g * (1.0 - sigma))
        gb[at] = w * swish
        return 0

    lax.fori_loop(0, NDEV, factors, 0)
    for j in range(2 * NK):
        pltpu.make_async_copy(
            wd_h.at[:, pl.ds(j * CH, CH)], wd.at[j], w_sem.at[2 + j]
        ).wait()
    raw[...] = jnp.zeros_like(raw)

    def add_raw(j):
        def part(r, _):
            at = pl.ds(pl.multiple_of(r * 384, 384), 384)
            blk = rows[j, pl.ds(r * 8, 8)].reshape(384, CH)
            raw[at] += dot(blk, wd[j], 1, 1)
            return 0

        lax.fori_loop(0, 4, part, 0)

    def arrive(k, _):
        mine = core * NK + k
        theirs = other * NK + k
        wait_bytes(rows.at[mine], d_recv.at[k])
        pltpu.make_async_remote_copy(
            src_ref=rows.at[mine], dst_ref=rows.at[mine], send_sem=s_send.at[k],
            recv_sem=s_recv.at[k], device_id=(sec, sib), device_id_type=MESH,
        ).start()
        add_raw(mine)
        wait_bytes(rows.at[theirs], s_recv.at[k])
        add_raw(theirs)
        return 0

    lax.fori_loop(0, NK, arrive, 0)

    def pre(b, _):
        at = pl.ds(pl.multiple_of(b * CAP, CAP), CAP)
        r = raw[at]
        dg[at] = (r * ga[at]).astype(BF)
        du[at] = (r * gb[at]).astype(BF)
        part = jnp.sum(r * hid[at], axis=1, keepdims=True)
        line = jnp.sum(jnp.where(diag, part, 0.0), axis=0, keepdims=True)
        gpsend[b] = jnp.broadcast_to(line, (8, TOK))
        return 0

    lax.fori_loop(0, NDEV, pre, 0)

    def partial_of(j, r):
        at = pl.ds(pl.multiple_of(r * 384, 384), 384)
        feat = pl.ds(pl.multiple_of(j * CH, CH), CH)
        return dot(dg[at], wg[feat], 1, 1) + dot(du[at], wu[feat], 1, 1)

    def to_sibling(k):
        slot = k % 2

        @pl.when(k >= 2)
        def _():
            wait_bytes(psend.at[slot], p_send.at[slot])

        def part(r, _):
            psend[slot, pl.ds(r * 8, 8)] = (
                partial_of(other * NK + k, r).astype(BF).reshape(8, CAP, CH)
            )
            return 0

        lax.fori_loop(0, 4, part, 0)
        pltpu.make_async_remote_copy(
            src_ref=psend.at[slot], dst_ref=comb.at[k], send_sem=p_send.at[slot],
            recv_sem=p_recv.at[k], device_id=(sec, sib), device_id_type=MESH,
        ).start()

    to_sibling(0)
    self_at = (chip % 2) * 8 + chip // 2

    def combine(k, _):
        @pl.when(k + 1 < NK)
        def _():
            to_sibling(k + 1)

        wait_bytes(comb.at[k], p_recv.at[k])

        def part(r, _):
            got = comb[k, pl.ds(r * 8, 8)].reshape(384, CH).astype(F32)
            comb[k, pl.ds(r * 8, 8)] = (
                (partial_of(core * NK + k, r) + got).astype(BF).reshape(8, CAP, CH)
            )
            return 0

        lax.fori_loop(0, 4, part, 0)

        def out(o, _):
            to = (chip + o) % NCHIP
            pltpu.make_async_remote_copy(
                src_ref=comb.at[k, pl.ds(to * 2, 2)],
                dst_ref=back.at[k, self_at],
                send_sem=c_send.at[k], recv_sem=c_recv.at[k],
                device_id=(sec, to * 2 + core), device_id_type=MESH,
            ).start()
            return 0

        lax.fori_loop(1, NCHIP, out, 0)
        pltpu.make_async_copy(
            comb.at[k, pl.ds(chip * 2, 2)], back.at[k, self_at], c_recv.at[k]
        ).start()
        return 0

    lax.fori_loop(0, NK, combine, 0)

    def sendgp(o, _):
        to = (me + o) % NDEV
        pltpu.make_async_remote_copy(
            src_ref=gpsend.at[to], dst_ref=gprecv.at[me], send_sem=gp_send,
            recv_sem=gp_recv, device_id=(sec, to), device_id_type=MESH,
        ).start()
        return 0

    lax.fori_loop(1, NDEV, sendgp, 0)
    pltpu.make_async_copy(gpsend.at[me], gprecv.at[me], gp_recv).start()

    def outs(slot, j):
        feat = pl.ds(pl.multiple_of(j * CH, CH), CH)
        return (
            pltpu.make_async_copy(st_d.at[slot], gwd_h.at[:, feat], o_sem.at[0, slot]),
            pltpu.make_async_copy(st_g.at[slot], gwg_h.at[feat], o_sem.at[1, slot]),
            pltpu.make_async_copy(st_u.at[slot], gwu_h.at[feat], o_sem.at[2, slot]),
        )

    def wgrad(j, _):
        slot = j % 2

        @pl.when(j >= 2)
        def _():
            for copy in outs(slot, j - 2):
                copy.wait()

        feat = pl.ds(pl.multiple_of(j * CH, CH), CH)
        st_d[slot] = dot(sh[...], rows[j].reshape(SLOTS, CH), 0, 0).astype(BF)
        st_g[slot] = dot(inputs[:, feat], dg[...], 0, 0).astype(BF)
        st_u[slot] = dot(inputs[:, feat], du[...], 0, 0).astype(BF)
        for copy in outs(slot, j):
            copy.start()
        return 0

    lax.fori_loop(0, 2 * NK, wgrad, 0)
    for j in (2 * NK - 2, 2 * NK - 1):
        for copy in outs(j % 2, j):
            copy.wait()

    def unpack(b, k):
        even = back[k, 0:8, b].reshape(EXPERTS * CAP, CH)
        odd = back[k, 8:16, b].reshape(EXPERTS * CAP, CH)
        return (dot(gmat[b], even, 1, 0) + dot(gmat[b], odd, 1, 0)).astype(BF)

    def final(k, _):
        wait_bytes(back.at[k], c_recv.at[k])
        gsib[k] = unpack(other, k)
        pltpu.make_async_remote_copy(
            src_ref=gsib.at[k], dst_ref=gout.at[core * NK + k], send_sem=gi_send,
            recv_sem=gi_recv.at[k], device_id=(sec, sib), device_id_type=MESH,
        ).start()
        gout[core * NK + k] = unpack(core, k)
        return 0

    lax.fori_loop(0, NK, final, 0)

    wait_bytes(gprecv, gp_recv)
    acc0 = jnp.zeros((TOK, TOK), F32)
    acc1 = jnp.zeros((TOK, TOK), F32)
    for e in range(EXPERTS):
        total = (
            gprecv[4 * e][0:1] + gprecv[4 * e + 1][0:1]
            + gprecv[4 * e + 2][0:1] + gprecv[4 * e + 3][0:1]
        )
        at = lane + e * CAP
        inside = lane < CAP
        acc0 = acc0 + jnp.where((at == tgt[0]) & inside, total, 0.0)
        acc1 = acc1 + jnp.where((at == tgt[1]) & inside, total, 0.0)
    gg_o[:, 0:1] = jnp.sum(acc0, axis=1, keepdims=True)
    gg_o[:, 1:2] = jnp.sum(acc1, axis=1, keepdims=True)

    def write(k, _):
        wait_bytes(gout.at[other * NK + k], gi_recv.at[k])
        return 0

    lax.fori_loop(0, NK, write, 0)
    for j in range(2 * NK):
        pltpu.make_async_copy(
            gout.at[j], gi_h.at[:, pl.ds(j * CH, CH)], go_sem.at[j]
        ).start()

    wait_bytes(xbuf, x_send)
    wait_bytes(gmat.at[0], gm_send)
    wait_bytes(grecv.at[pl.ds(0, NDEV - 1)], g_send)
    wait_bytes(gprecv.at[pl.ds(0, NDEV - 1)], gp_send)
    wait_bytes(gsib, gi_send)

    def drain(k, _):
        wait_bytes(rows.at[k, pl.ds(0, 30)], d_send.at[k])
        wait_bytes(comb.at[k, pl.ds(0, 30)], c_send.at[k])
        wait_bytes(rows.at[k], s_send.at[k])
        return 0

    lax.fori_loop(0, NK, drain, 0)
    for slot in range(2):
        wait_bytes(psend.at[slot], p_send.at[slot])
    for j in range(2 * NK):
        pltpu.make_async_copy(
            gout.at[j], gi_h.at[:, pl.ds(j * CH, CH)], go_sem.at[j]
        ).wait()


def local(nsec, upstream, routes, gates, w_gate, w_up, w_down, stash_q, stash_scale):
    hbm = pl.BlockSpec(memory_space=pl.ANY)
    vmem = pl.BlockSpec(memory_space=pltpu.VMEM)
    dma = pltpu.SemaphoreType.DMA
    v = pltpu.VMEM
    scratch = [
        v((2 * NK, NDEV, CAP, CH), BF),
        v((SLOTS, D), BF),
        v((D, FD), BF), v((D, FD), BF), v((2 * NK, FD, CH), BF),
        v((SLOTS, FD), F32), v((SLOTS, FD), F32), v((SLOTS, FD), F32), v((SLOTS, FD), F32),
        v((SLOTS, FD), BF), v((SLOTS, FD), BF), v((SLOTS, FD), BF),
        v((NK, EXPERTS, 2, CAP, CH), BF),
        v((NK, 2, TOK, CH), BF),
        v((NK, NDEV, CAP, CH), BF),
        v((2, NDEV, CAP, CH), BF),
        v((NK, NCHIP, 2, CAP, CH), BF),
        v((2 * NK, TOK, CH), BF), v((NK, TOK, CH), BF),
        v((SLOTS, D // 128), F32),
        v((2, TOK, EXPERTS * CAP), BF),
        v((2, TOK, TOK), jnp.int32),
        v((EXPERTS, 8, TOK), F32), v((NDEV, 8, TOK), F32),
        v((NDEV, 8, TOK), F32), v((NDEV, 8, TOK), F32),
        v((2, FD, CH), BF), v((2, CH, FD), BF), v((2, CH, FD), BF),
        dma, dma((NK,)), dma((NK,)), dma((NK,)), dma((NK,)), dma((NK,)),
        dma((2,)), dma((NK,)), dma((NK,)), dma((NK,)), dma, dma, dma, dma, dma, dma,
        dma, dma((NK,)), dma((2 + 2 * NK,)), dma((NFR,)), dma, dma((3, 2)), dma((2 * NK,)),
    ]
    out = pl.pallas_call(
        functools.partial(kernel, nsec),
        out_shape=(
            jax.ShapeDtypeStruct((TOK, D), BF),
            jax.ShapeDtypeStruct((TOK, 2), F32),
            jax.ShapeDtypeStruct((D, FD), BF),
            jax.ShapeDtypeStruct((D, FD), BF),
            jax.ShapeDtypeStruct((FD, D), BF),
        ),
        in_specs=[vmem, vmem] + [hbm] * 6,
        out_specs=(hbm, vmem, hbm, hbm, hbm),
        scratch_shapes=scratch,
        compiler_params=pltpu.CompilerParams(
            collective_id=0, has_side_effects=True, vmem_limit_bytes=66_000_000
        ),
    )(
        routes[0], gates[0], upstream[0], w_gate[0], w_up[0], w_down[0],
        stash_q[0], stash_scale[0],
    )
    return tuple(o[None] for o in out)


def solution(mesh):
    three = P("section", "expert", None)
    cols = P("section", None, "expert")
    return jax.shard_map(
        functools.partial(local, mesh.shape["section"]),
        mesh=mesh,
        in_specs=(three, three, three, cols, cols, three, three, three),
        out_specs=(three, three, cols, cols, three),
        check_vma=False,
    )
```

```python
import functools

import jax
import jax.numpy as jnp
from jax import lax
from jax.experimental import pallas as pl
from jax.experimental.pallas import tpu as pltpu
from jax.sharding import PartitionSpec as P

EXPERTS = 8
CAP = 48
NCHIP = 16
NDEV = 32
CH = 256
D = 3584
HALF = D // 2
NK = HALF // CH
SLOTS = NDEV * CAP
FD = 256
TOK = 128
NFR = 8
HSLOTS = SLOTS // 2
PART = HSLOTS // 2
MESH = pl.DeviceIdType.MESH
BF = jnp.bfloat16
F32 = jnp.float32


def dot(a, b, ca, cb):
    return lax.dot_general(a, b, (((ca,), (cb,)), ((), ())), preferred_element_type=F32)


def wait_bytes(ref, sem):
    pltpu.make_async_copy(ref, ref, sem).wait()


def kernel(
    nsec,
    routes, gates, up, wg_h, wu_h, wd_h, sq_h, ss_h,
    gi_h, gg_o, gwg_h, gwu_h, gwd_h,
    rows, inputs, wg, wu, wd, ga, gb, hid, raw, sh, dg, du,
    send, xbuf, comb, psend, back, gout, gsib, scale, scale_t, gmat, tgt,
    gsend, grecv, gpsend, gprecv, st_d, st_g, st_u,
    x_send, x_recv, d_send, d_recv, s_send, s_recv, p_send, p_recv,
    c_send, c_recv, gm_send, gm_recv, g_send, g_recv, gp_send, gp_recv,
    gi_send, gi_recv, w_sem, sq_sem, ss_sem, o_sem, go_sem,
):
    sec = lax.axis_index("section")
    me = lax.axis_index("expert")
    chip = me // 2
    core = me % 2
    sib = me + 1 - 2 * core
    other = 1 - core
    down = (sec + nsec - 1) % nsec
    upper = (sec + 1) % nsec

    pltpu.make_async_copy(ss_h, scale, ss_sem).start()

    def stash(f):
        return pltpu.make_async_copy(
            sq_h.at[pl.ds((f % 4) * 4, 4), f // 4],
            inputs.at[f // 4, pl.ds((f % 4) * 4, 4)],
            sq_sem.at[f],
        )

    for f in range(NFR):
        stash(f).start()
    pltpu.make_async_copy(wg_h, wg, w_sem.at[0]).start()
    pltpu.make_async_copy(wu_h, wu, w_sem.at[1]).start()
    for j in range(2 * NK):
        pltpu.make_async_copy(wd_h.at[:, pl.ds(j * CH, CH)], wd.at[j], w_sem.at[2 + j]).start()

    bar = pltpu.get_barrier_semaphore()

    def greet(o, _):
        pl.semaphore_signal(
            bar, inc=1, device_id=(sec, (me + o) % NDEV), device_id_type=MESH
        )
        return 0

    lax.fori_loop(1, NDEV, greet, 0)
    for sx in (down, upper):
        for cc in range(2):
            pl.semaphore_signal(
                bar, inc=1, device_id=(sx, chip * 2 + cc), device_id_type=MESH
            )

    lane = lax.broadcasted_iota(jnp.int32, (TOK, TOK), 1)
    sub = lax.broadcasted_iota(jnp.int32, (TOK, TOK), 0)
    same = lane == sub

    def column(row):
        return jnp.sum(jnp.where(same, row, 0), axis=1, keepdims=True)

    r0 = column(routes[0:1, :])
    r1 = column(routes[1:2, :])
    w0 = column(gates[0:1, :])
    w1 = column(gates[1:2, :])
    o0 = (lane == r0).astype(F32)
    o1 = (lane == r1).astype(F32)
    lower = (lane < sub).astype(BF)
    before = dot(lower, (o0 + o1).astype(BF), 1, 0)
    t0 = r0 * CAP + jnp.sum(before * o0, axis=1, keepdims=True).astype(jnp.int32)
    t1 = r1 * CAP + jnp.sum(before * o1, axis=1, keepdims=True).astype(jnp.int32)
    tgt[0] = jnp.broadcast_to(t0, (TOK, TOK))
    tgt[1] = jnp.broadcast_to(t1, (TOK, TOK))
    wide = lax.broadcasted_iota(jnp.int32, (TOK, EXPERTS * CAP), 1)
    gmat[core] = ((wide == t0) | (wide == t1)).astype(F32).astype(BF)
    for e in range(EXPERTS):
        at = lane + e * CAP
        inside = lane < CAP
        hit = jnp.where((at == t0) & inside, w0, 0.0) + jnp.where((at == t1) & inside, w1, 0.0)
        gsend[e] = jnp.broadcast_to(jnp.sum(hit, axis=0, keepdims=True), (8, TOK))

    pl.semaphore_wait(bar, NDEV - 1 + 4)

    def xs(k, _):
        for cc in range(2):
            pltpu.make_async_remote_copy(
                src_ref=up.at[:, pl.ds(pl.multiple_of(cc * HALF + k * CH, CH), CH)],
                dst_ref=xbuf.at[k, core],
                send_sem=x_send,
                recv_sem=x_recv.at[k],
                device_id=(down, chip * 2 + cc),
                device_id_type=MESH,
            ).start()
        return 0

    pltpu.make_async_remote_copy(
        src_ref=gmat.at[core], dst_ref=gmat.at[core], send_sem=gm_send, recv_sem=gm_recv,
        device_id=(sec, sib), device_id_type=MESH,
    ).start()
    lax.fori_loop(0, NK, xs, 0)

    def sendg(o, _):
        to = (me + o) % NDEV
        pltpu.make_async_remote_copy(
            src_ref=gsend.at[to // 4], dst_ref=grecv.at[me], send_sem=g_send,
            recv_sem=g_recv, device_id=(sec, to), device_id_type=MESH,
        ).start()
        return 0

    lax.fori_loop(1, NDEV, sendg, 0)
    pltpu.make_async_copy(gsend.at[me // 4], grecv.at[me], g_recv).start()

    pltpu.make_async_copy(ss_h, scale, ss_sem).wait()
    for q in range(4):
        for m in range(3):
            at = slice(q * 384 + m * 128, q * 384 + (m + 1) * 128)
            lines = [scale[n, :, at] for n in range(D // 128)]
            lines.append(jnp.zeros((4, 128), F32))
            scale_t[at, :] = jnp.concatenate(lines, axis=0).T
    wait_bytes(gmat.at[0], gm_recv)

    pltpu.make_async_copy(wg_h, wg, w_sem.at[0]).wait()
    pltpu.make_async_copy(wu_h, wu, w_sem.at[1]).wait()

    def spread(h, k):
        def out(o, _):
            to = (chip + o) % NCHIP
            pltpu.make_async_remote_copy(
                src_ref=send.at[k, h, to // 2],
                dst_ref=rows.at[core * NK + k, h, chip],
                send_sem=d_send.at[h * NK + k], recv_sem=d_recv.at[h * NK + k],
                device_id=(sec, to * 2 + core), device_id_type=MESH,
            ).start()
            return 0

        lax.fori_loop(1, NCHIP, out, 0)
        pltpu.make_async_copy(
            send.at[k, h, chip // 2], rows.at[core * NK + k, h, chip], d_recv.at[h * NK + k]
        ).start()

    def forward(f):
        h = f // 4
        c4 = (f % 4) * 4
        stash(f).wait()

        def dequant(q, _):
            chp = c4 + q
            sc = scale_t[pl.ds(pl.multiple_of((chp * 2 + h) * CAP, CAP), CAP), :]
            for n in range(D // 128):
                cols = slice(n * 128, (n + 1) * 128)
                v = inputs[h, chp, :, cols].astype(F32) * sc[:, n : n + 1]
                inputs[h, chp, :, cols] = v.astype(BF)
            return 0

        lax.fori_loop(0, 4, dequant, 0)
        at = pl.ds(pl.multiple_of(f * 4 * CAP, 4 * CAP), 4 * CAP)
        block = inputs[h, pl.ds(c4, 4)].reshape(4 * CAP, D)
        ga[at] = dot(block, wg[...], 1, 0)
        gb[at] = dot(block, wu[...], 1, 0)

    def dispatch(k, _):
        wait_bytes(xbuf.at[k], x_recv.at[k])
        for b in range(2):
            packed = dot(gmat[b], xbuf[k, b], 0, 0).astype(BF)
            send[k, b] = packed.reshape(EXPERTS, CAP, CH)
        spread(0, k)
        forward(k)
        return 0

    lax.fori_loop(0, NK, dispatch, 0)

    def dispatch1(k, _):
        spread(1, k)
        return 0

    lax.fori_loop(0, NK, dispatch1, 0)
    forward(NK)

    wait_bytes(grecv, g_recv)
    diag = lax.broadcasted_iota(jnp.int32, (CAP, TOK), 0) == lax.broadcasted_iota(
        jnp.int32, (CAP, TOK), 1
    )

    def factors(b, _):
        at = pl.ds(pl.multiple_of(b * CAP, CAP), CAP)
        source = (b % NCHIP) * 2 + b // NCHIP
        w = jnp.sum(jnp.where(diag, grecv[source][0:1], 0.0), axis=1, keepdims=True)
        g = ga[at]
        u = gb[at]
        sigma = jax.nn.sigmoid(g)
        swish = g * sigma
        h = swish * u
        hid[at] = h
        sh[at] = (w * h).astype(BF)
        ga[at] = w * u * sigma * (1.0 + g * (1.0 - sigma))
        gb[at] = w * swish
        return 0

    lax.fori_loop(0, NDEV, factors, 0)
    for j in range(2 * NK):
        pltpu.make_async_copy(
            wd_h.at[:, pl.ds(j * CH, CH)], wd.at[j], w_sem.at[2 + j]
        ).wait()
    raw[...] = jnp.zeros_like(raw)

    def add_raw(h, j):
        def part(r, _):
            at = pl.ds(pl.multiple_of(h * HSLOTS + r * PART, PART), PART)
            blk = rows[j, h, pl.ds(r * 8, 8)].reshape(PART, CH)
            raw[at] += dot(blk, wd[j], 1, 1)
            return 0

        lax.fori_loop(0, 2, part, 0)

    def arrive(h, k):
        mine = core * NK + k
        theirs = other * NK + k
        t = h * NK + k
        wait_bytes(rows.at[mine, h], d_recv.at[t])
        pltpu.make_async_remote_copy(
            src_ref=rows.at[mine, h], dst_ref=rows.at[mine, h], send_sem=s_send.at[t],
            recv_sem=s_recv.at[t], device_id=(sec, sib), device_id_type=MESH,
        ).start()
        add_raw(h, mine)
        wait_bytes(rows.at[theirs, h], s_recv.at[t])
        add_raw(h, theirs)

    def pre(b, _):
        at = pl.ds(pl.multiple_of(b * CAP, CAP), CAP)
        r = raw[at]
        dg[at] = (r * ga[at]).astype(BF)
        du[at] = (r * gb[at]).astype(BF)
        part = jnp.sum(r * hid[at], axis=1, keepdims=True)
        line = jnp.sum(jnp.where(diag, part, 0.0), axis=0, keepdims=True)
        gpsend[(b % NCHIP) * 2 + b // NCHIP] = jnp.broadcast_to(line, (8, TOK))
        return 0

    def partial_of(h, j, r):
        at = pl.ds(pl.multiple_of(h * HSLOTS + r * PART, PART), PART)
        feat = pl.ds(pl.multiple_of(j * CH, CH), CH)
        return dot(dg[at], wg[feat], 1, 1) + dot(du[at], wu[feat], 1, 1)

    def to_sibling(h, k):
        t = h * NK + k
        slot = t % 2

        @pl.when(t >= 2)
        def _():
            wait_bytes(psend.at[slot], p_send.at[slot])

        def part(r, _):
            psend[slot, pl.ds(r * 8, 8)] = (
                partial_of(h, other * NK + k, r).astype(BF).reshape(8, CAP, CH)
            )
            return 0

        lax.fori_loop(0, 2, part, 0)
        pltpu.make_async_remote_copy(
            src_ref=psend.at[slot], dst_ref=comb.at[h, k], send_sem=p_send.at[slot],
            recv_sem=p_recv.at[t], device_id=(sec, sib), device_id_type=MESH,
        ).start()

    self_at = (chip % 2) * 8 + chip // 2

    def combine(h, k):
        t = h * NK + k

        @pl.when(k + 1 < NK)
        def _():
            to_sibling(h, k + 1)

        wait_bytes(comb.at[h, k], p_recv.at[t])

        def part(r, _):
            got = comb[h, k, pl.ds(r * 8, 8)].reshape(PART, CH).astype(F32)
            comb[h, k, pl.ds(r * 8, 8)] = (
                (partial_of(h, core * NK + k, r) + got).astype(BF).reshape(8, CAP, CH)
            )
            return 0

        lax.fori_loop(0, 2, part, 0)

        def out(o, _):
            to = (chip + o) % NCHIP
            pltpu.make_async_remote_copy(
                src_ref=comb.at[h, k, to],
                dst_ref=back.at[h, k, self_at],
                send_sem=c_send.at[t], recv_sem=c_recv.at[t],
                device_id=(sec, to * 2 + core), device_id_type=MESH,
            ).start()
            return 0

        lax.fori_loop(1, NCHIP, out, 0)
        pltpu.make_async_copy(
            comb.at[h, k, chip], back.at[h, k, self_at], c_recv.at[t]
        ).start()

    def half(h, _):
        def arrivals(k, _):
            arrive(h, k)
            return 0

        lax.fori_loop(0, NK, arrivals, 0)
        lax.fori_loop(h * NCHIP, h * NCHIP + NCHIP, pre, 0)
        to_sibling(h, 0)

        def combines(k, _):
            combine(h, k)
            return 0

        lax.fori_loop(0, NK, combines, 0)
        return 0

    lax.fori_loop(0, 2, half, 0)

    def sendgp(o, _):
        to = (me + o) % NDEV
        pltpu.make_async_remote_copy(
            src_ref=gpsend.at[to], dst_ref=gprecv.at[me], send_sem=gp_send,
            recv_sem=gp_recv, device_id=(sec, to), device_id_type=MESH,
        ).start()
        return 0

    lax.fori_loop(1, NDEV, sendgp, 0)
    pltpu.make_async_copy(gpsend.at[me], gprecv.at[me], gp_recv).start()

    def outs(slot, j):
        feat = pl.ds(pl.multiple_of(j * CH, CH), CH)
        return (
            pltpu.make_async_copy(st_d.at[slot], gwd_h.at[:, feat], o_sem.at[0, slot]),
            pltpu.make_async_copy(st_g.at[slot], gwg_h.at[feat], o_sem.at[1, slot]),
            pltpu.make_async_copy(st_u.at[slot], gwu_h.at[feat], o_sem.at[2, slot]),
        )

    def wgrad(j, _):
        slot = j % 2

        @pl.when(j >= 2)
        def _():
            for copy in outs(slot, j - 2):
                copy.wait()

        feat = pl.ds(pl.multiple_of(j * CH, CH), CH)
        st_d[slot] = dot(sh[...], rows[j].reshape(SLOTS, CH), 0, 0).astype(BF)
        xin = inputs[:, :, :, feat].reshape(SLOTS, CH)
        st_g[slot] = dot(xin, dg[...], 0, 0).astype(BF)
        st_u[slot] = dot(xin, du[...], 0, 0).astype(BF)
        for copy in outs(slot, j):
            copy.start()
        return 0

    lax.fori_loop(0, 2 * NK, wgrad, 0)
    for j in (2 * NK - 2, 2 * NK - 1):
        for copy in outs(j % 2, j):
            copy.wait()

    def final(h, k):
        wait_bytes(back.at[h, k], c_recv.at[h * NK + k])
        even = back[h, k, 0:8].reshape(EXPERTS * CAP, CH)
        odd = back[h, k, 8:16].reshape(EXPERTS * CAP, CH)
        got = (dot(gmat[h], even, 1, 0) + dot(gmat[h], odd, 1, 0)).astype(BF)

        @pl.when(core == h)
        def _():
            gout[core * NK + k] = got

        @pl.when(core != h)
        def _():
            gsib[k] = got
            pltpu.make_async_remote_copy(
                src_ref=gsib.at[k], dst_ref=gout.at[core * NK + k], send_sem=gi_send,
                recv_sem=gi_recv.at[k], device_id=(sec, sib), device_id_type=MESH,
            ).start()

    for h in range(2):

        def finals(k, _):
            final(h, k)
            return 0

        lax.fori_loop(0, NK, finals, 0)

    def put(j):
        return pltpu.make_async_copy(
            gout.at[j], gi_h.at[:, pl.ds(pl.multiple_of(j * CH, CH), CH)], go_sem.at[j]
        )

    def write(k, _):
        put(core * NK + k).start()
        return 0

    lax.fori_loop(0, NK, write, 0)

    wait_bytes(gprecv, gp_recv)
    acc0 = jnp.zeros((TOK, TOK), F32)
    acc1 = jnp.zeros((TOK, TOK), F32)
    for e in range(EXPERTS):
        total = (
            gprecv[4 * e][0:1] + gprecv[4 * e + 1][0:1]
            + gprecv[4 * e + 2][0:1] + gprecv[4 * e + 3][0:1]
        )
        at = lane + e * CAP
        inside = lane < CAP
        acc0 = acc0 + jnp.where((at == tgt[0]) & inside, total, 0.0)
        acc1 = acc1 + jnp.where((at == tgt[1]) & inside, total, 0.0)
    for n, acc in enumerate((acc0, acc1)):
        part = jnp.sum(acc, axis=1, keepdims=True)
        gg_o[n : n + 1, :] = jnp.sum(jnp.where(same, part, 0.0), axis=0, keepdims=True)

    def write_sib(k, _):
        wait_bytes(gout.at[other * NK + k], gi_recv.at[k])
        put(other * NK + k).start()
        return 0

    lax.fori_loop(0, NK, write_sib, 0)

    wait_bytes(xbuf, x_send)
    wait_bytes(gmat.at[0], gm_send)
    wait_bytes(grecv.at[pl.ds(0, NDEV - 1)], g_send)
    wait_bytes(gprecv.at[pl.ds(0, NDEV - 1)], gp_send)
    wait_bytes(gsib, gi_send)

    def drain(t, _):
        wait_bytes(rows.at[0, 0, pl.ds(0, NCHIP - 1)], d_send.at[t])
        wait_bytes(comb.at[0, 0, pl.ds(0, NCHIP - 1)], c_send.at[t])
        wait_bytes(rows.at[0, 0], s_send.at[t])
        put(t).wait()
        return 0

    lax.fori_loop(0, 2 * NK, drain, 0)
    for slot in range(2):
        wait_bytes(psend.at[slot], p_send.at[slot])


def emit(*refs):
    count = (len(refs) - 1) // 3
    srcs, dsts, bufs, sem = refs[:count], refs[count : 2 * count], refs[2 * count : -1], refs[-1]
    loads, stores = [], []
    n = 0
    for src, dst, buf in zip(srcs, dsts, bufs):
        size = src.shape[0]
        pieces = 4 if size >= 64 else 1
        for p in range(pieces):
            at = pl.ds(p * (size // pieces), size // pieces)
            loads.append(pltpu.make_async_copy(src.at[at], buf.at[at], sem.at[0, n]))
            stores.append(pltpu.make_async_copy(buf.at[at], dst.at[at], sem.at[1, n]))
            n += 1
    for load in loads:
        load.start()
    for load, store in zip(loads, stores):
        load.wait()
        store.start()
    for store in stores:
        store.wait()


def local(nsec, upstream, routes, gates, w_gate, w_up, w_down, stash_q, stash_scale):
    hbm = pl.BlockSpec(memory_space=pl.ANY)
    vmem = pl.BlockSpec(memory_space=pltpu.VMEM)
    dma = pltpu.SemaphoreType.DMA
    v = pltpu.VMEM
    both = 2 * NK
    scratch = [
        v((both, 2, NCHIP, CAP, CH), BF),
        v((2, NCHIP, CAP, D), BF),
        v((D, FD), BF), v((D, FD), BF), v((both, FD, CH), BF),
        v((SLOTS, FD), F32), v((SLOTS, FD), F32), v((SLOTS, FD), F32), v((SLOTS, FD), F32),
        v((SLOTS, FD), BF), v((SLOTS, FD), BF), v((SLOTS, FD), BF),
        v((NK, 2, EXPERTS, CAP, CH), BF),
        v((NK, 2, TOK, CH), BF),
        v((2, NK, NCHIP, CAP, CH), BF),
        v((2, NCHIP, CAP, CH), BF),
        v((2, NK, NCHIP, CAP, CH), BF),
        v((both, TOK, CH), BF), v((NK, TOK, CH), BF),
        v((D // 128, 1, SLOTS), F32), v((SLOTS, 32), F32),
        v((2, TOK, EXPERTS * CAP), BF),
        v((2, TOK, TOK), jnp.int32),
        v((EXPERTS, 8, TOK), F32), v((NDEV, 8, TOK), F32),
        v((NDEV, 8, TOK), F32), v((NDEV, 8, TOK), F32),
        v((2, FD, CH), BF), v((2, CH, FD), BF), v((2, CH, FD), BF),
        dma, dma((NK,)), dma((both,)), dma((both,)), dma((both,)), dma((both,)),
        dma((2,)), dma((both,)), dma((both,)), dma((both,)), dma, dma, dma, dma, dma, dma,
        dma, dma((NK,)), dma((2 + both,)), dma((NFR,)), dma, dma((3, 2)), dma((both,)),
    ]
    shapes = (
        jax.ShapeDtypeStruct((TOK, D), BF),
        jax.ShapeDtypeStruct((2, TOK), F32),
        jax.ShapeDtypeStruct((D, FD), BF),
        jax.ShapeDtypeStruct((D, FD), BF),
        jax.ShapeDtypeStruct((FD, D), BF),
    )
    out = pl.pallas_call(
        functools.partial(kernel, nsec),
        out_shape=shapes,
        in_specs=[vmem, vmem] + [hbm] * 6,
        out_specs=(hbm, vmem, hbm, hbm, hbm),
        scratch_shapes=scratch,
        compiler_params=pltpu.CompilerParams(
            collective_id=0, has_side_effects=True, vmem_limit_bytes=66_000_000
        ),
    )(
        routes[0].T, gates[0].T, upstream[0], w_gate[0], w_up[0], w_down[0],
        stash_q.reshape(NCHIP, 2, CAP, D), jnp.transpose(stash_scale, (2, 0, 1)),
    )
    out = pl.pallas_call(
        emit,
        out_shape=shapes,
        in_specs=[hbm] * 5,
        out_specs=(hbm,) * 5,
        scratch_shapes=[v(o.shape, o.dtype) for o in shapes] + [dma((2, 20))],
        compiler_params=pltpu.CompilerParams(vmem_limit_bytes=64_000_000),
    )(*out)
    gi, gg, gwg, gwu, gwd = out
    return gi[None], gg.T[None], gwg[None], gwu[None], gwd[None]


def solution(mesh):
    three = P("section", "expert", None)
    cols = P("section", None, "expert")
    return jax.shard_map(
        functools.partial(local, mesh.shape["section"]),
        mesh=mesh,
        in_specs=(three, three, three, cols, cols, three, three, three),
        out_specs=(three, three, cols, cols, three),
        check_vma=False,
    )
```

```python
import functools

import jax
import jax.numpy as jnp
from jax import lax
from jax.experimental import pallas as pl
from jax.experimental.pallas import tpu as pltpu
from jax.sharding import PartitionSpec as P

EXPERTS = 8
CAP = 48
NCHIP = 16
NDEV = 32
CH = 256
D = 3584
HALF = D // 2
NK = HALF // CH
NZ = 3
NY = NK - NZ
SIDE = 4
SLOTS = NDEV * CAP
FD = 256
TOK = 128
NFR = 8
HSLOTS = SLOTS // 2
PART = HSLOTS // 2
MESH = pl.DeviceIdType.MESH
BF = jnp.bfloat16
F32 = jnp.float32


def dot(a, b, ca, cb):
    return lax.dot_general(a, b, (((ca,), (cb,)), ((), ())), preferred_element_type=F32)


def wait_bytes(ref, sem):
    pltpu.make_async_copy(ref, ref, sem).wait()


def kernel(
    nsec,
    routes, gates, up, wg_h, wu_h, wd_h, sq_h, ss_h,
    gi_h, gg_o, gwg_h, gwu_h, gwd_h,
    rows, inputs, wgu, wd, ga, gb, hid, sh, dgu,
    zsend, zbuf, ybuf, ysend, xbuf, comb, psend, cbuf, backz, ybk, ytok, gout, gsib,
    scale, scale_t, gmat, gmat_t, gy, gy_t, tgt, trow, trows,
    gsend, grecv, gpsend, gprecv, st_d, st_g, st_u,
    x_send, x_recv, f_send, f_recv, d_send, d_recv, s_send, s_recv, p_send, p_recv,
    q_send, q_recv, c_send, c_recv, t_send, t_recv, g_send, g_recv, gp_send, gp_recv,
    gi_send, gi_recv, w_sem, sq_sem, ss_sem, o_sem, go_sem,
):
    sec = lax.axis_index("section")
    me = lax.axis_index("expert")
    chip = me // 2
    core = me % 2
    sib = me + 1 - 2 * core
    other = 1 - core
    down = (sec + nsec - 1) % nsec
    upper = (sec + 1) % nsec
    z = chip // SIDE
    y = chip % SIDE
    pair = y // 2

    def chunk(i):
        return i // 2 + NZ * (1 - i % 2)

    def send_to(src, dst, ssem, rsem, dev):
        pltpu.make_async_remote_copy(
            src_ref=src, dst_ref=dst, send_sem=ssem, recv_sem=rsem,
            device_id=(sec, dev), device_id_type=MESH,
        ).start()

    def at_z(zz):
        return (zz * SIDE + y) * 2 + core

    def at_y(yy):
        return (z * SIDE + yy) * 2 + core

    def others(body):
        def step(o, _):
            body(o)
            return 0

        lax.fori_loop(1, SIDE, step, 0)

    def feat(j):
        return pl.ds(pl.multiple_of(j * CH, CH), CH)

    def block(h, j):
        return rows.at[h, :, :, :, feat(j)]

    def loop(lo, hi, *steps):
        def body(i, _):
            for step in steps:
                step(i)
            return 0

        lax.fori_loop(lo, hi, body, 0)

    def by_type(i, do_y, do_z):
        if isinstance(i, int):
            (do_z if i % 2 else do_y)(i // 2)
            return

        @pl.when(i % 2 == 0)
        def _():
            do_y(i // 2)

        @pl.when(i % 2 == 1)
        def _():
            do_z(i // 2)

    pltpu.make_async_copy(ss_h, scale, ss_sem).start()

    def stash(f):
        return pltpu.make_async_copy(
            sq_h.at[pl.ds((f % 4) * 4, 4), f // 4],
            inputs.at[f // 4, pl.ds((f % 4) * 4, 4)],
            sq_sem.at[f],
        )

    for f in range(NFR):
        stash(f).start()
    weights = (
        pltpu.make_async_copy(wg_h, wgu.at[:, pl.ds(0, FD)], w_sem.at[0]),
        pltpu.make_async_copy(wu_h, wgu.at[:, pl.ds(FD, FD)], w_sem.at[1]),
        pltpu.make_async_copy(wd_h, wd, w_sem.at[2]),
    )
    for copy in weights:
        copy.start()

    bar = pltpu.get_barrier_semaphore()

    def greet(o, _):
        pl.semaphore_signal(
            bar, inc=1, device_id=(sec, (me + o) % NDEV), device_id_type=MESH
        )
        return 0

    lax.fori_loop(1, NDEV, greet, 0)
    for sx in (down, upper):
        for cc in range(2):
            pl.semaphore_signal(
                bar, inc=1, device_id=(sx, chip * 2 + cc), device_id_type=MESH
            )

    lane = lax.broadcasted_iota(jnp.int32, (TOK, TOK), 1)
    sub = lax.broadcasted_iota(jnp.int32, (TOK, TOK), 0)
    same = lane == sub

    def column(row):
        return jnp.sum(jnp.where(same, row, 0), axis=1, keepdims=True)

    r0 = column(routes[0:1, :])
    r1 = column(routes[1:2, :])
    w0 = column(gates[0:1, :])
    w1 = column(gates[1:2, :])
    o0 = (lane == r0).astype(F32)
    o1 = (lane == r1).astype(F32)
    lower = (lane < sub).astype(BF)
    before = dot(lower, (o0 + o1).astype(BF), 1, 0)
    t0 = r0 * CAP + jnp.sum(before * o0, axis=1, keepdims=True).astype(jnp.int32)
    t1 = r1 * CAP + jnp.sum(before * o1, axis=1, keepdims=True).astype(jnp.int32)
    tgt[0] = jnp.broadcast_to(t0, (TOK, TOK))
    tgt[1] = jnp.broadcast_to(t1, (TOK, TOK))
    trow[...] = jnp.zeros_like(trow)
    for n, t in enumerate((t0, t1)):
        line = jnp.sum(jnp.where(same, t, 0), axis=0, keepdims=True)
        trow[n : n + 1, :] = line.astype(F32)
    for e in range(EXPERTS):
        at = lane + e * CAP
        inside = lane < CAP
        hit = jnp.where((at == t0) & inside, w0, 0.0) + jnp.where((at == t1) & inside, w1, 0.0)
        gsend[e] = jnp.broadcast_to(jnp.sum(hit, axis=0, keepdims=True), (8, TOK))

    pl.semaphore_wait(bar, NDEV - 1 + 4)

    def xs(i):
        k = chunk(i)
        for cc in range(2):
            pltpu.make_async_remote_copy(
                src_ref=up.at[:, pl.ds(pl.multiple_of(cc * HALF + k * CH, CH), CH)],
                dst_ref=xbuf.at[k, core],
                send_sem=x_send,
                recv_sem=x_recv.at[core * NK + k],
                device_id=(down, chip * 2 + cc),
                device_id_type=MESH,
            ).start()

    @pl.when(core == 0)
    def _():
        loop(0, NK, xs)

    spot = me % 8

    def send_rows(o, _):
        to = z * 8 + (spot + o) % 8
        send_to(trow, trows.at[spot], t_send, t_recv, to)
        return 0

    lax.fori_loop(1, 8, send_rows, 0)
    pltpu.make_async_copy(trow, trows.at[spot], t_recv).start()
    def sendg(o, _):
        to = (me + o) % NDEV
        pltpu.make_async_remote_copy(
            src_ref=gsend.at[to // 4], dst_ref=grecv.at[me], send_sem=g_send,
            recv_sem=g_recv, device_id=(sec, to), device_id_type=MESH,
        ).start()
        return 0

    lax.fori_loop(1, NDEV, sendg, 0)
    pltpu.make_async_copy(gsend.at[me // 4], grecv.at[me], g_recv).start()

    def arrived(h, i):
        k = chunk(i)
        wait_bytes(xbuf.at[k, h], x_recv.at[h * NK + k])

    def first_y(h, ky):
        src = xbuf.at[NZ + ky, h]
        dst = ybuf.at[ky, h, y]
        t = h * NK + NZ + ky
        others(lambda o: send_to(src, dst, f_send.at[t], f_recv.at[t], at_y((y + o) % SIDE)))
        pltpu.make_async_copy(src, dst, f_recv.at[t]).start()

    def first_z(h, kz):
        packed = dot(gmat_t[h], xbuf[kz, h], 1, 0).astype(BF)
        zsend[kz, h] = packed.reshape(SIDE, 2, CAP, CH)
        dst = zbuf.at[kz, h, z]
        t = h * NK + kz

        def out(o):
            to = (z + o) % SIDE
            send_to(zsend.at[kz, h, to], dst, f_send.at[t], f_recv.at[t], at_z(to))

        others(out)
        pltpu.make_async_copy(zsend.at[kz, h, z], dst, f_recv.at[t]).start()

    def first(h, i):
        arrived(h, i)
        by_type(i, functools.partial(first_y, h), functools.partial(first_z, h))

    first(0, 0)

    pltpu.make_async_copy(ss_h, scale, ss_sem).wait()
    for q in range(4):
        for m in range(3):
            at = slice(q * 384 + m * 128, q * 384 + (m + 1) * 128)
            lines = [scale[n, :, at] for n in range(D // 128)]
            lines.append(jnp.zeros((4, 128), F32))
            scale_t[at, :] = jnp.concatenate(lines, axis=0).T

    wait_bytes(trows, t_recv)

    def hits(t, axis, size, positions):
        shape = (size, TOK) if axis == 0 else (TOK, size)
        at = positions(lax.broadcasted_iota(jnp.int32, shape, axis))
        lines = [t[n : n + 1].astype(jnp.int32) for n in range(2)]
        if axis == 1:
            lines = [column(line) for line in lines]
        return ((at == lines[0]) | (at == lines[1])).astype(F32).astype(BF)

    def all_slots(at):
        return at

    def pair_slots(at):
        step = sum((at >= n * CAP).astype(jnp.int32) for n in range(1, SIDE))
        return at + (step + pair) * CAP

    for b in range(2):
        t = trows[y * 2 + b]
        gmat[b] = hits(t, 1, EXPERTS * CAP, all_slots)
        gmat_t[b] = hits(t, 0, EXPERTS * CAP, all_slots)
        for n in range(SIDE):
            t = trows[n * 2 + b]
            gy[b, n] = hits(t, 1, SIDE * CAP, pair_slots)
            gy_t[b, n] = hits(t, 0, SIDE * CAP, pair_slots)


    weights[0].wait()
    weights[1].wait()

    def second(h, i):
        k = chunk(i)
        t = h * NK + k
        j = core * NK + k

        def do_y(ky):
            wait_bytes(ybuf.at[ky, h], f_recv.at[t])
            for n in range(SIDE):
                packed = dot(gy_t[h, n], ybuf[ky, h, n], 1, 0).astype(BF)
                ysend[ky, h, :, n] = packed.reshape(SIDE, CAP, CH)
            dst = rows.at[h, z, :, :, feat(j)]

            def out(o):
                to = (z + o) % SIDE
                send_to(ysend.at[ky, h, to], dst, d_send.at[t], d_recv.at[t], at_z(to))

            others(out)
            pltpu.make_async_copy(ysend.at[ky, h, z], dst, d_recv.at[t]).start()

        def do_z(kz):
            wait_bytes(zbuf.at[kz, h], f_recv.at[t])
            dst = rows.at[h, :, y, :, feat(j)]

            def out(o):
                to = (y + o) % SIDE
                send_to(
                    zbuf.at[kz, h, :, to // 2], dst, d_send.at[t], d_recv.at[t], at_y(to)
                )

            others(out)
            pltpu.make_async_copy(zbuf.at[kz, h, :, pair], dst, d_recv.at[t]).start()

        by_type(i, do_y, do_z)

    def forward(f):
        h = f // 4
        c4 = (f % 4) * 4
        stash(f).wait()

        def dequant(q, _):
            chp = c4 + q
            sc = scale_t[pl.ds(pl.multiple_of((chp * 2 + h) * CAP, CAP), CAP), :]
            for n in range(D // 128):
                cols = slice(n * 128, (n + 1) * 128)
                v = inputs[h, chp, :, cols].astype(F32) * sc[:, n : n + 1]
                inputs[h, chp, :, cols] = v.astype(BF)
            return 0

        lax.fori_loop(0, 4, dequant, 0)
        at = pl.ds(pl.multiple_of(f * 4 * CAP, 4 * CAP), 4 * CAP)
        both = dot(inputs[h, pl.ds(c4, 4)].reshape(4 * CAP, D), wgu[...], 1, 0)
        ga[at] = both[:, :FD]
        gb[at] = both[:, FD:]

    def dispatch(i):
        first(0, i)

        @pl.when((core == 1) & (i == 2))
        def _():
            loop(0, NK, xs)

        forward(i)
        second(0, i - 1)

    forward(0)
    loop(1, NK, dispatch)
    second(0, NK - 1)
    loop(0, NK, lambda i: first(1, i))
    forward(NK)

    wait_bytes(grecv, g_recv)
    diag = lax.broadcasted_iota(jnp.int32, (CAP, TOK), 0) == lax.broadcasted_iota(
        jnp.int32, (CAP, TOK), 1
    )

    def factors(b, _):
        at = pl.ds(pl.multiple_of(b * CAP, CAP), CAP)
        source = (b % NCHIP) * 2 + b // NCHIP
        w = jnp.sum(jnp.where(diag, grecv[source][0:1], 0.0), axis=1, keepdims=True)
        g = ga[at]
        u = gb[at]
        sigma = jax.nn.sigmoid(g)
        swish = g * sigma
        h = swish * u
        hid[at] = h
        sh[at] = (w * h).astype(BF)
        ga[at] = w * u * sigma * (1.0 + g * (1.0 - sigma))
        gb[at] = w * swish
        return 0

    lax.fori_loop(0, NDEV, factors, 0)

    def pass_on(h, i):
        k = chunk(i)
        t = h * NK + k
        mine = block(h, core * NK + k)
        wait_bytes(mine, d_recv.at[t])
        send_to(mine, mine, s_send.at[t], s_recv.at[t], sib)

    def settle(h, i):
        k = chunk(i)
        wait_bytes(block(h, other * NK + k), s_recv.at[h * NK + k])

    def pre(h, zz):
        at = pl.ds(pl.multiple_of(h * HSLOTS + zz * SIDE * CAP, SIDE * CAP), SIDE * CAP)
        r = dot(rows[h, zz].reshape(SIDE * CAP, D), wd[...], 1, 1)
        dgu[at, 0:FD] = (r * ga[at]).astype(BF)
        dgu[at, FD : 2 * FD] = (r * gb[at]).astype(BF)
        part = jnp.sum(r * hid[at], axis=1, keepdims=True)
        for n in range(SIDE):
            piece = part[n * CAP : (n + 1) * CAP]
            line = jnp.sum(jnp.where(diag, piece, 0.0), axis=0, keepdims=True)
            gpsend[(zz * SIDE + n) * 2 + h] = jnp.broadcast_to(line, (8, TOK))

    def partial_of(h, j, r):
        at = pl.ds(pl.multiple_of(h * HSLOTS + r * PART, PART), PART)
        return dot(dgu[at], wgu[feat(j)], 1, 1)

    def to_sibling(h, i):
        k = chunk(i)
        turn = h * NK + i
        slot = turn % 2

        @pl.when(turn >= 2)
        def _():
            wait_bytes(psend.at[slot], p_send.at[slot])

        def part(r, _):
            psend[slot, pl.ds(r * 2, 2)] = (
                partial_of(h, other * NK + k, r).astype(BF).reshape(2, SIDE, CAP, CH)
            )
            return 0

        lax.fori_loop(0, 2, part, 0)
        send_to(
            psend.at[slot], comb.at[h, k], p_send.at[slot], p_recv.at[h * NK + k], sib
        )

    def combine(h, i):
        k = chunk(i)
        t = h * NK + k

        @pl.when(i + 1 < NK)
        def _():
            to_sibling(h, i + 1)

        wait_bytes(comb.at[h, k], p_recv.at[t])

        def part(r, _):
            got = comb[h, k, pl.ds(r * 2, 2)].reshape(PART, CH).astype(F32)
            comb[h, k, pl.ds(r * 2, 2)] = (
                (partial_of(h, core * NK + k, r) + got).astype(BF).reshape(2, SIDE, CAP, CH)
            )
            return 0

        lax.fori_loop(0, 2, part, 0)

        def do_y(ky):
            dst = ybk.at[h, ky, z]

            def out(o):
                to = (z + o) % SIDE
                send_to(comb.at[h, k, to], dst, q_send.at[t], q_recv.at[t], at_z(to))

            others(out)
            pltpu.make_async_copy(comb.at[h, k, z], dst, q_recv.at[t]).start()

        def do_z(kz):
            dst = cbuf.at[h, kz, y]

            def out(o):
                to = (y + o) % SIDE
                send_to(comb.at[h, k, :, to], dst, q_send.at[t], q_recv.at[t], at_y(to))

            others(out)
            pltpu.make_async_copy(comb.at[h, k, :, y], dst, q_recv.at[t]).start()

        by_type(i, do_y, do_z)

    def relay(h, i):
        t = h * NK + chunk(i)

        def do_y(ky):
            wait_bytes(ybk.at[h, ky], q_recv.at[t])
            for n in range(SIDE):
                mat = ybk[h, ky, :, n].reshape(SIDE * CAP, CH)
                ybuf[ky, h, n] = dot(gy[h, n], mat, 1, 0).astype(BF)
            dst = ytok.at[h, ky, y]

            def out(o):
                to = (y + o) % SIDE
                send_to(ybuf.at[ky, h, to], dst, c_send.at[t], c_recv.at[t], at_y(to))

            others(out)
            pltpu.make_async_copy(ybuf.at[ky, h, y], dst, c_recv.at[t]).start()

        def do_z(kz):
            wait_bytes(cbuf.at[h, kz], q_recv.at[t])
            wait_bytes(comb.at[0, 0, pl.ds(0, SIDE - 1)], d_send.at[t])
            for n in range(2):
                total = cbuf[h, kz, 2 * n].astype(F32) + cbuf[h, kz, 2 * n + 1].astype(F32)
                zbuf[kz, h, :, n] = total.astype(BF)
            dst = backz.at[h, kz, z]

            def out(o):
                to = (z + o) % SIDE
                send_to(zbuf.at[kz, h, to], dst, c_send.at[t], c_recv.at[t], at_z(to))

            others(out)
            pltpu.make_async_copy(zbuf.at[kz, h, z], dst, c_recv.at[t]).start()

        by_type(i, do_y, do_z)

    def outs(slot, j):
        return (
            pltpu.make_async_copy(st_d.at[slot], gwd_h.at[:, feat(j)], o_sem.at[0, slot]),
            pltpu.make_async_copy(st_g.at[slot], gwg_h.at[feat(j)], o_sem.at[1, slot]),
            pltpu.make_async_copy(st_u.at[slot], gwu_h.at[feat(j)], o_sem.at[2, slot]),
        )

    def wgrad(j):
        slot = j % 2

        @pl.when(j >= 2)
        def _():
            for copy in outs(slot, j - 2):
                copy.wait()

        st_d[slot] = dot(sh[...], rows[:, :, :, :, feat(j)].reshape(SLOTS, CH), 0, 0).astype(BF)
        xin = inputs[:, :, :, feat(j)].reshape(SLOTS, CH)
        both = dot(xin, dgu[...], 0, 0)
        st_g[slot] = both[:, :FD].astype(BF)
        st_u[slot] = both[:, FD:].astype(BF)
        for copy in outs(slot, j):
            copy.start()

    def send_part(o):
        to = (me + o) % NDEV
        send_to(gpsend.at[to], gprecv.at[me], gp_send, gp_recv, to)

    loop(0, NK, lambda i: pass_on(0, i), lambda i: second(1, i))
    weights[2].wait()
    loop(0, NK, lambda i: settle(0, i))
    loop(0, SIDE, lambda n: pre(0, n))
    to_sibling(0, 0)
    loop(0, NK, lambda i: combine(0, i), lambda i: pass_on(1, i))
    loop(0, NK, lambda i: settle(1, i))
    loop(0, SIDE, lambda n: pre(1, n))
    to_sibling(1, 0)
    loop(0, NK, lambda i: combine(1, i), lambda i: relay(0, i))
    loop(1, NDEV, send_part)
    pltpu.make_async_copy(gpsend.at[me], gprecv.at[me], gp_recv).start()
    loop(
        0, NK, lambda i: wgrad(2 * i), lambda i: relay(1, i), lambda i: wgrad(2 * i + 1)
    )
    for j in (2 * NK - 2, 2 * NK - 1):
        for copy in outs(j % 2, j):
            copy.wait()

    def final(h, i):
        k = chunk(i)
        t = h * NK + k

        def hand(got):
            @pl.when(core == h)
            def _():
                gout[core * NK + k] = got

            @pl.when(core != h)
            def _():
                gsib[k] = got
                send_to(gsib.at[k], gout.at[core * NK + k], gi_send, gi_recv.at[k], sib)

        def do_y(ky):
            wait_bytes(ytok.at[h, ky], c_recv.at[t])
            hand(sum(ytok[h, ky, n].astype(F32) for n in range(SIDE)).astype(BF))

        def do_z(kz):
            wait_bytes(backz.at[h, kz], c_recv.at[t])
            mat = backz[h, kz].reshape(EXPERTS * CAP, CH)
            hand(dot(gmat[h], mat, 1, 0).astype(BF))

        by_type(i, do_y, do_z)

    for h in range(2):

        def finals(k, _):
            final(h, k)
            return 0

        lax.fori_loop(0, NK, finals, 0)

    def put(j):
        return pltpu.make_async_copy(
            gout.at[j], gi_h.at[:, pl.ds(pl.multiple_of(j * CH, CH), CH)], go_sem.at[j]
        )

    def write(k, _):
        put(core * NK + k).start()
        return 0

    lax.fori_loop(0, NK, write, 0)

    wait_bytes(gprecv, gp_recv)
    acc0 = jnp.zeros((TOK, TOK), F32)
    acc1 = jnp.zeros((TOK, TOK), F32)
    for e in range(EXPERTS):
        total = (
            gprecv[4 * e][0:1] + gprecv[4 * e + 1][0:1]
            + gprecv[4 * e + 2][0:1] + gprecv[4 * e + 3][0:1]
        )
        at = lane + e * CAP
        inside = lane < CAP
        acc0 = acc0 + jnp.where((at == tgt[0]) & inside, total, 0.0)
        acc1 = acc1 + jnp.where((at == tgt[1]) & inside, total, 0.0)
    for n, acc in enumerate((acc0, acc1)):
        part = jnp.sum(acc, axis=1, keepdims=True)
        gg_o[n : n + 1, :] = jnp.sum(jnp.where(same, part, 0.0), axis=0, keepdims=True)

    def write_sib(k, _):
        wait_bytes(gout.at[other * NK + k], gi_recv.at[k])
        put(other * NK + k).start()
        return 0

    lax.fori_loop(0, NK, write_sib, 0)

    wait_bytes(xbuf, x_send)
    wait_bytes(trows.at[pl.ds(0, 7)], t_send)
    wait_bytes(grecv.at[pl.ds(0, NDEV - 1)], g_send)
    wait_bytes(gprecv.at[pl.ds(0, NDEV - 1)], gp_send)
    wait_bytes(gsib, gi_send)

    def drain(t, _):
        wait_bytes(comb.at[0, 0, pl.ds(0, SIDE - 1)], q_send.at[t])
        wait_bytes(comb.at[0, 0], s_send.at[t])

        @pl.when(t % NK >= NZ)
        def _():
            wait_bytes(comb.at[0, 0, pl.ds(0, SIDE - 1)], d_send.at[t])
            wait_bytes(ybuf.at[0, 0, pl.ds(0, SIDE - 1)], f_send.at[t])
            wait_bytes(ybuf.at[0, 0, pl.ds(0, SIDE - 1)], c_send.at[t])

        @pl.when(t % NK < NZ)
        def _():
            wait_bytes(zbuf.at[0, 0, pl.ds(0, SIDE - 1)], f_send.at[t])
            wait_bytes(zbuf.at[0, 0, pl.ds(0, SIDE - 1)], c_send.at[t])

        put(t).wait()
        return 0

    lax.fori_loop(0, 2 * NK, drain, 0)
    for slot in range(2):
        wait_bytes(psend.at[slot], p_send.at[slot])


def emit(*refs):
    count = (len(refs) - 1) // 3
    srcs, dsts, bufs, sem = refs[:count], refs[count : 2 * count], refs[2 * count : -1], refs[-1]
    loads, stores = [], []
    n = 0
    for src, dst, buf in zip(srcs, dsts, bufs):
        size = src.shape[0]
        pieces = 4 if size >= 64 else 1
        for p in range(pieces):
            at = pl.ds(p * (size // pieces), size // pieces)
            loads.append(pltpu.make_async_copy(src.at[at], buf.at[at], sem.at[0, n]))
            stores.append(pltpu.make_async_copy(buf.at[at], dst.at[at], sem.at[1, n]))
            n += 1
    for load in loads:
        load.start()
    for load, store in zip(loads, stores):
        load.wait()
        store.start()
    for store in stores:
        store.wait()


def local(nsec, upstream, routes, gates, w_gate, w_up, w_down, stash_q, stash_scale):
    hbm = pl.BlockSpec(memory_space=pl.ANY)
    vmem = pl.BlockSpec(memory_space=pltpu.VMEM)
    dma = pltpu.SemaphoreType.DMA
    v = pltpu.VMEM
    both = 2 * NK
    scratch = [
        v((2, SIDE, SIDE, CAP, D), BF),
        v((2, NCHIP, CAP, D), BF),
        v((D, 2 * FD), BF), v((FD, D), BF),
        v((SLOTS, FD), F32), v((SLOTS, FD), F32), v((SLOTS, FD), F32),
        v((SLOTS, FD), BF), v((SLOTS, 2 * FD), BF),
        v((NZ, 2, SIDE, 2, CAP, CH), BF), v((NZ, 2, SIDE, 2, CAP, CH), BF),
        v((NY, 2, SIDE, TOK, CH), BF), v((NY, 2, SIDE, SIDE, CAP, CH), BF),
        v((NK, 2, TOK, CH), BF),
        v((2, NK, SIDE, SIDE, CAP, CH), BF),
        v((2, SIDE, SIDE, CAP, CH), BF),
        v((2, NZ, SIDE, SIDE, CAP, CH), BF), v((2, NZ, SIDE, 2, CAP, CH), BF),
        v((2, NY, SIDE, SIDE, CAP, CH), BF), v((2, NY, SIDE, TOK, CH), BF),
        v((both, TOK, CH), BF), v((NK, TOK, CH), BF),
        v((D // 128, 1, SLOTS), F32), v((SLOTS, 32), F32),
        v((2, TOK, EXPERTS * CAP), BF), v((2, EXPERTS * CAP, TOK), BF),
        v((2, SIDE, TOK, SIDE * CAP), BF), v((2, SIDE, SIDE * CAP, TOK), BF),
        v((2, TOK, TOK), jnp.int32),
        v((8, TOK), F32), v((8, 8, TOK), F32),
        v((EXPERTS, 8, TOK), F32), v((NDEV, 8, TOK), F32),
        v((NDEV, 8, TOK), F32), v((NDEV, 8, TOK), F32),
        v((2, FD, CH), BF), v((2, CH, FD), BF), v((2, CH, FD), BF),
        dma, dma((both,)), dma((both,)), dma((both,)), dma((both,)), dma((both,)),
        dma((both,)), dma((both,)), dma((2,)), dma((both,)), dma((both,)), dma((both,)),
        dma((both,)), dma((both,)), dma, dma, dma, dma, dma, dma,
        dma, dma((NK,)), dma((3,)), dma((NFR,)), dma, dma((3, 2)), dma((both,)),
    ]
    shapes = (
        jax.ShapeDtypeStruct((TOK, D), BF),
        jax.ShapeDtypeStruct((2, TOK), F32),
        jax.ShapeDtypeStruct((D, FD), BF),
        jax.ShapeDtypeStruct((D, FD), BF),
        jax.ShapeDtypeStruct((FD, D), BF),
    )
    out = pl.pallas_call(
        functools.partial(kernel, nsec),
        out_shape=shapes,
        in_specs=[vmem, vmem] + [hbm] * 6,
        out_specs=(hbm, vmem, hbm, hbm, hbm),
        scratch_shapes=scratch,
        compiler_params=pltpu.CompilerParams(
            collective_id=0, has_side_effects=True, vmem_limit_bytes=67_043_328
        ),
    )(
        routes[0].T, gates[0].T, upstream[0], w_gate[0], w_up[0], w_down[0],
        stash_q.reshape(NCHIP, 2, CAP, D), jnp.transpose(stash_scale, (2, 0, 1)),
    )
    out = pl.pallas_call(
        emit,
        out_shape=shapes,
        in_specs=[hbm] * 5,
        out_specs=(hbm,) * 5,
        scratch_shapes=[v(o.shape, o.dtype) for o in shapes] + [dma((2, 20))],
        compiler_params=pltpu.CompilerParams(vmem_limit_bytes=64_000_000),
    )(*out)
    gi, gg, gwg, gwu, gwd = out
    return gi[None], gg.T[None], gwg[None], gwu[None], gwd[None]


def solution(mesh):
    three = P("section", "expert", None)
    cols = P("section", None, "expert")
    return jax.shard_map(
        functools.partial(local, mesh.shape["section"]),
        mesh=mesh,
        in_specs=(three, three, three, cols, cols, three, three, three),
        out_specs=(three, three, cols, cols, three),
        check_vma=False,
    )
```

```python
import functools

import jax
import jax.numpy as jnp
from jax import lax
from jax.experimental import pallas as pl
from jax.experimental.pallas import tpu as pltpu
from jax.sharding import PartitionSpec as P

EXPERTS = 8
CAP = 48
NCHIP = 16
NDEV = 32
CH = 256
D = 3584
HALF = D // 2
NK = HALF // CH
NZ = 3
NY = NK - NZ
SIDE = 4
SLOTS = NDEV * CAP
FD = 256
TOK = 128
NFR = 8
HSLOTS = SLOTS // 2
PART = HSLOTS // 2
MESH = pl.DeviceIdType.MESH
BF = jnp.bfloat16
F32 = jnp.float32


def dot(a, b, ca, cb):
    return lax.dot_general(a, b, (((ca,), (cb,)), ((), ())), preferred_element_type=F32)


def wait_bytes(ref, sem):
    pltpu.make_async_copy(ref, ref, sem).wait()


def kernel(
    nsec,
    routes_h, gates_h, up, wg_h, wu_h, wd_h, sq_h, ss_h,
    gi_h, gg_o, gwg_h, gwu_h, gwd_h,
    routes, gates, rows, inputs, wgu, wd, ga, gb, hid, sh, dgu,
    zsend, zbuf, ybuf, ysend, xbuf, comb, psend, cbuf, backz, ybk, ytok, gout, gsib,
    scale, scale_t, gmat, gmat_t, gy, gy_t, tgt, trow, trows,
    gsend, grecv, gpsend, gprecv, st_d, st_g, st_u,
    x_send, x_recv, f_send, f_recv, d_send, d_recv, s_send, s_recv, p_send, p_recv,
    q_send, q_recv, c_send, c_recv, t_send, t_recv, g_send, g_recv, gp_send, gp_recv,
    gi_send, gi_recv, w_sem, sq_sem, ss_sem, o_sem, go_sem, l_sem,
):
    sec = lax.axis_index("section")
    me = lax.axis_index("expert")
    chip = me // 2
    core = me % 2
    sib = me + 1 - 2 * core
    other = 1 - core
    down = (sec + nsec - 1) % nsec
    upper = (sec + 1) % nsec
    z = chip // SIDE
    y = chip % SIDE
    pair = y // 2

    def chunk(i):
        return i // 2 + NZ * (1 - i % 2)

    def send_to(src, dst, ssem, rsem, dev):
        pltpu.make_async_remote_copy(
            src_ref=src, dst_ref=dst, send_sem=ssem, recv_sem=rsem,
            device_id=(sec, dev), device_id_type=MESH,
        ).start()

    def at_z(zz):
        return (zz * SIDE + y) * 2 + core

    def at_y(yy):
        return (z * SIDE + yy) * 2 + core

    def others(body):
        def step(o, _):
            body(o)
            return 0

        lax.fori_loop(1, SIDE, step, 0)

    def feat(j):
        return pl.ds(pl.multiple_of(j * CH, CH), CH)

    def block(h, j):
        return rows.at[h, :, :, :, feat(j)]

    def loop(lo, hi, *steps):
        def body(i, _):
            for step in steps:
                step(i)
            return 0

        lax.fori_loop(lo, hi, body, 0)

    def by_type(i, do_y, do_z):
        if isinstance(i, int):
            (do_z if i % 2 else do_y)(i // 2)
            return

        @pl.when(i % 2 == 0)
        def _():
            do_y(i // 2)

        @pl.when(i % 2 == 1)
        def _():
            do_z(i // 2)

    bar = pltpu.get_barrier_semaphore()

    def greet(o, _):
        pl.semaphore_signal(
            bar, inc=1, device_id=(sec, (me + o) % NDEV), device_id_type=MESH
        )
        return 0

    lax.fori_loop(1, NDEV, greet, 0)
    for sx in (down, upper):
        for cc in range(2):
            pl.semaphore_signal(
                bar, inc=1, device_id=(sx, chip * 2 + cc), device_id_type=MESH
            )

    small = (
        pltpu.make_async_copy(routes_h, routes, l_sem.at[0]),
        pltpu.make_async_copy(gates_h, gates, l_sem.at[1]),
    )
    for copy in small:
        copy.start()
    pltpu.make_async_copy(ss_h, scale, ss_sem).start()

    def stash(f):
        return pltpu.make_async_copy(
            sq_h.at[pl.ds((f % 4) * 4, 4), f // 4],
            inputs.at[f // 4, pl.ds((f % 4) * 4, 4)],
            sq_sem.at[f],
        )

    for f in range(NFR):
        stash(f).start()
    weights = (
        pltpu.make_async_copy(wg_h, wgu.at[:, pl.ds(0, FD)], w_sem.at[0]),
        pltpu.make_async_copy(wu_h, wgu.at[:, pl.ds(FD, FD)], w_sem.at[1]),
        pltpu.make_async_copy(wd_h, wd, w_sem.at[2]),
    )
    for copy in weights:
        copy.start()

    pl.semaphore_wait(bar, NDEV - 1 + 4)

    def xs(i):
        k = chunk(i)
        for cc in range(2):
            pltpu.make_async_remote_copy(
                src_ref=up.at[:, pl.ds(pl.multiple_of(cc * HALF + k * CH, CH), CH)],
                dst_ref=xbuf.at[k, core],
                send_sem=x_send,
                recv_sem=x_recv.at[core * NK + k],
                device_id=(down, chip * 2 + cc),
                device_id_type=MESH,
            ).start()

    @pl.when(core == 0)
    def _():
        loop(0, NK, xs)

    for copy in small:
        copy.wait()

    lane = lax.broadcasted_iota(jnp.int32, (TOK, TOK), 1)
    sub = lax.broadcasted_iota(jnp.int32, (TOK, TOK), 0)
    same = lane == sub

    def column(row):
        return jnp.sum(jnp.where(same, row, 0), axis=1, keepdims=True)

    r0 = column(routes[0:1, :])
    r1 = column(routes[1:2, :])
    w0 = column(gates[0:1, :])
    w1 = column(gates[1:2, :])
    o0 = (lane == r0).astype(F32)
    o1 = (lane == r1).astype(F32)
    lower = (lane < sub).astype(BF)
    before = dot(lower, (o0 + o1).astype(BF), 1, 0)
    t0 = r0 * CAP + jnp.sum(before * o0, axis=1, keepdims=True).astype(jnp.int32)
    t1 = r1 * CAP + jnp.sum(before * o1, axis=1, keepdims=True).astype(jnp.int32)
    tgt[0] = jnp.broadcast_to(t0, (TOK, TOK))
    tgt[1] = jnp.broadcast_to(t1, (TOK, TOK))
    trow[...] = jnp.zeros_like(trow)
    for n, t in enumerate((t0, t1)):
        line = jnp.sum(jnp.where(same, t, 0), axis=0, keepdims=True)
        trow[n : n + 1, :] = line.astype(F32)
    for e in range(EXPERTS):
        at = lane + e * CAP
        inside = lane < CAP
        hit = jnp.where((at == t0) & inside, w0, 0.0) + jnp.where((at == t1) & inside, w1, 0.0)
        gsend[e] = jnp.broadcast_to(jnp.sum(hit, axis=0, keepdims=True), (8, TOK))

    spot = me % 8

    def send_rows(o, _):
        to = z * 8 + (spot + o) % 8
        send_to(trow, trows.at[spot], t_send, t_recv, to)
        return 0

    lax.fori_loop(1, 8, send_rows, 0)
    pltpu.make_async_copy(trow, trows.at[spot], t_recv).start()
    def sendg(o, _):
        to = (me + o) % NDEV
        pltpu.make_async_remote_copy(
            src_ref=gsend.at[to // 4], dst_ref=grecv.at[me], send_sem=g_send,
            recv_sem=g_recv, device_id=(sec, to), device_id_type=MESH,
        ).start()
        return 0

    lax.fori_loop(1, NDEV, sendg, 0)
    pltpu.make_async_copy(gsend.at[me // 4], grecv.at[me], g_recv).start()

    def arrived(h, i):
        k = chunk(i)
        wait_bytes(xbuf.at[k, h], x_recv.at[h * NK + k])

    def first_y(h, ky):
        src = xbuf.at[NZ + ky, h]
        dst = ybuf.at[ky, h, y]
        t = h * NK + NZ + ky
        others(lambda o: send_to(src, dst, f_send.at[t], f_recv.at[t], at_y((y + o) % SIDE)))
        pltpu.make_async_copy(src, dst, f_recv.at[t]).start()

    def first_z(h, kz):
        packed = dot(gmat_t[h], xbuf[kz, h], 1, 0).astype(BF)
        zsend[kz, h] = packed.reshape(SIDE, 2, CAP, CH)
        dst = zbuf.at[kz, h, z]
        t = h * NK + kz

        def out(o):
            to = (z + o) % SIDE
            send_to(zsend.at[kz, h, to], dst, f_send.at[t], f_recv.at[t], at_z(to))

        others(out)
        pltpu.make_async_copy(zsend.at[kz, h, z], dst, f_recv.at[t]).start()

    def first(h, i):
        arrived(h, i)
        by_type(i, functools.partial(first_y, h), functools.partial(first_z, h))

    first(0, 0)

    wait_bytes(trows, t_recv)

    def hits(t, axis, size, positions):
        shape = (size, TOK) if axis == 0 else (TOK, size)
        at = positions(lax.broadcasted_iota(jnp.int32, shape, axis))
        lines = [t[n : n + 1].astype(jnp.int32) for n in range(2)]
        if axis == 1:
            lines = [column(line) for line in lines]
        return ((at == lines[0]) | (at == lines[1])).astype(F32).astype(BF)

    def all_slots(at):
        return at

    def pair_slots(at):
        step = sum((at >= n * CAP).astype(jnp.int32) for n in range(1, SIDE))
        return at + (step + pair) * CAP

    for b in range(2):
        gmat_t[b] = hits(trows[y * 2 + b], 0, EXPERTS * CAP, all_slots)
        for n in range(SIDE):
            gy_t[b, n] = hits(trows[n * 2 + b], 0, SIDE * CAP, pair_slots)


    def second(h, i):
        k = chunk(i)
        t = h * NK + k
        j = core * NK + k

        def do_y(ky):
            wait_bytes(ybuf.at[ky, h], f_recv.at[t])
            for n in range(SIDE):
                packed = dot(gy_t[h, n], ybuf[ky, h, n], 1, 0).astype(BF)
                ysend[ky, h, :, n] = packed.reshape(SIDE, CAP, CH)
            dst = rows.at[h, z, :, :, feat(j)]

            def out(o):
                to = (z + o) % SIDE
                send_to(ysend.at[ky, h, to], dst, d_send.at[t], d_recv.at[t], at_z(to))

            others(out)
            pltpu.make_async_copy(ysend.at[ky, h, z], dst, d_recv.at[t]).start()

        def do_z(kz):
            wait_bytes(zbuf.at[kz, h], f_recv.at[t])
            dst = rows.at[h, :, y, :, feat(j)]

            def out(o):
                to = (y + o) % SIDE
                send_to(
                    zbuf.at[kz, h, :, to // 2], dst, d_send.at[t], d_recv.at[t], at_y(to)
                )

            others(out)
            pltpu.make_async_copy(zbuf.at[kz, h, :, pair], dst, d_recv.at[t]).start()

        by_type(i, do_y, do_z)

    def forward(f):
        h = f // 4
        c4 = (f % 4) * 4
        stash(f).wait()

        def dequant(q, _):
            chp = c4 + q
            sc = scale_t[pl.ds(pl.multiple_of((chp * 2 + h) * CAP, CAP), CAP), :]
            for n in range(D // 128):
                cols = slice(n * 128, (n + 1) * 128)
                v = inputs[h, chp, :, cols].astype(F32) * sc[:, n : n + 1]
                inputs[h, chp, :, cols] = v.astype(BF)
            return 0

        lax.fori_loop(0, 4, dequant, 0)
        at = pl.ds(pl.multiple_of(f * 4 * CAP, 4 * CAP), 4 * CAP)
        both = dot(inputs[h, pl.ds(c4, 4)].reshape(4 * CAP, D), wgu[...], 1, 0)
        ga[at] = both[:, :FD]
        gb[at] = both[:, FD:]

    loop(1, 5, lambda i: first(0, i))

    @pl.when(core == 1)
    def _():
        loop(0, NK, xs)

    second(0, 0)

    pltpu.make_async_copy(ss_h, scale, ss_sem).wait()
    for q in range(4):
        for m in range(3):
            at = slice(q * 384 + m * 128, q * 384 + (m + 1) * 128)
            lines = [scale[n, :, at] for n in range(D // 128)]
            lines.append(jnp.zeros((4, 128), F32))
            scale_t[at, :] = jnp.concatenate(lines, axis=0).T

    for b in range(2):
        gmat[b] = hits(trows[y * 2 + b], 1, EXPERTS * CAP, all_slots)
        for n in range(SIDE):
            gy[b, n] = hits(trows[n * 2 + b], 1, SIDE * CAP, pair_slots)
    weights[0].wait()
    weights[1].wait()
    first(0, 5)
    second(0, 1)
    forward(0)
    first(0, 6)
    second(0, 2)
    forward(1)
    loop(3, NK, lambda i: second(0, i), lambda i: first(1, i - 3), lambda i: forward(i - 1))
    loop(4, NK, lambda i: first(1, i))
    loop(6, NFR, forward)

    wait_bytes(grecv, g_recv)
    diag = lax.broadcasted_iota(jnp.int32, (CAP, TOK), 0) == lax.broadcasted_iota(
        jnp.int32, (CAP, TOK), 1
    )

    def factors(b, _):
        at = pl.ds(pl.multiple_of(b * CAP, CAP), CAP)
        source = (b % NCHIP) * 2 + b // NCHIP
        w = jnp.sum(jnp.where(diag, grecv[source][0:1], 0.0), axis=1, keepdims=True)
        g = ga[at]
        u = gb[at]
        sigma = jax.nn.sigmoid(g)
        swish = g * sigma
        h = swish * u
        hid[at] = h
        sh[at] = (w * h).astype(BF)
        ga[at] = w * u * sigma * (1.0 + g * (1.0 - sigma))
        gb[at] = w * swish
        return 0

    lax.fori_loop(0, NDEV, factors, 0)

    def pass_on(h, i):
        k = chunk(i)
        t = h * NK + k
        mine = block(h, core * NK + k)
        wait_bytes(mine, d_recv.at[t])
        send_to(mine, mine, s_send.at[t], s_recv.at[t], sib)

    def settle(h, i):
        k = chunk(i)
        wait_bytes(block(h, other * NK + k), s_recv.at[h * NK + k])

    def pre(h, zz):
        at = pl.ds(pl.multiple_of(h * HSLOTS + zz * SIDE * CAP, SIDE * CAP), SIDE * CAP)
        r = dot(rows[h, zz].reshape(SIDE * CAP, D), wd[...], 1, 1)
        dgu[at, 0:FD] = (r * ga[at]).astype(BF)
        dgu[at, FD : 2 * FD] = (r * gb[at]).astype(BF)
        part = jnp.sum(r * hid[at], axis=1, keepdims=True)
        for n in range(SIDE):
            piece = part[n * CAP : (n + 1) * CAP]
            line = jnp.sum(jnp.where(diag, piece, 0.0), axis=0, keepdims=True)
            gpsend[(zz * SIDE + n) * 2 + h] = jnp.broadcast_to(line, (8, TOK))

    def partial_of(h, j, r):
        at = pl.ds(pl.multiple_of(h * HSLOTS + r * PART, PART), PART)
        return dot(dgu[at], wgu[feat(j)], 1, 1)

    def to_sibling(h, i):
        k = chunk(i)
        turn = h * NK + i
        slot = turn % 2

        @pl.when(turn >= 2)
        def _():
            wait_bytes(psend.at[slot], p_send.at[slot])

        def part(r, _):
            psend[slot, pl.ds(r * 2, 2)] = (
                partial_of(h, other * NK + k, r).astype(BF).reshape(2, SIDE, CAP, CH)
            )
            return 0

        lax.fori_loop(0, 2, part, 0)
        send_to(
            psend.at[slot], comb.at[h, k], p_send.at[slot], p_recv.at[h * NK + k], sib
        )

    def combine(h, i):
        k = chunk(i)
        t = h * NK + k

        @pl.when(i + 1 < NK)
        def _():
            to_sibling(h, i + 1)

        wait_bytes(comb.at[h, k], p_recv.at[t])

        def part(r, _):
            got = comb[h, k, pl.ds(r * 2, 2)].reshape(PART, CH).astype(F32)
            comb[h, k, pl.ds(r * 2, 2)] = (
                (partial_of(h, core * NK + k, r) + got).astype(BF).reshape(2, SIDE, CAP, CH)
            )
            return 0

        lax.fori_loop(0, 2, part, 0)

        def do_y(ky):
            dst = ybk.at[h, ky, z]

            def out(o):
                to = (z + o) % SIDE
                send_to(comb.at[h, k, to], dst, q_send.at[t], q_recv.at[t], at_z(to))

            others(out)
            pltpu.make_async_copy(comb.at[h, k, z], dst, q_recv.at[t]).start()

        def do_z(kz):
            dst = cbuf.at[h, kz, y]

            def out(o):
                to = (y + o) % SIDE
                send_to(comb.at[h, k, :, to], dst, q_send.at[t], q_recv.at[t], at_y(to))

            others(out)
            pltpu.make_async_copy(comb.at[h, k, :, y], dst, q_recv.at[t]).start()

        by_type(i, do_y, do_z)

    def relay(h, i):
        t = h * NK + chunk(i)

        def do_y(ky):
            wait_bytes(ybk.at[h, ky], q_recv.at[t])
            for n in range(SIDE):
                mat = ybk[h, ky, :, n].reshape(SIDE * CAP, CH)
                ybuf[ky, h, n] = dot(gy[h, n], mat, 1, 0).astype(BF)
            dst = ytok.at[h, ky, y]

            def out(o):
                to = (y + o) % SIDE
                send_to(ybuf.at[ky, h, to], dst, c_send.at[t], c_recv.at[t], at_y(to))

            others(out)
            pltpu.make_async_copy(ybuf.at[ky, h, y], dst, c_recv.at[t]).start()

        def do_z(kz):
            wait_bytes(cbuf.at[h, kz], q_recv.at[t])
            wait_bytes(comb.at[0, 0, pl.ds(0, SIDE - 1)], d_send.at[t])
            for n in range(2):
                total = cbuf[h, kz, 2 * n].astype(F32) + cbuf[h, kz, 2 * n + 1].astype(F32)
                zbuf[kz, h, :, n] = total.astype(BF)
            dst = backz.at[h, kz, z]

            def out(o):
                to = (z + o) % SIDE
                send_to(zbuf.at[kz, h, to], dst, c_send.at[t], c_recv.at[t], at_z(to))

            others(out)
            pltpu.make_async_copy(zbuf.at[kz, h, z], dst, c_recv.at[t]).start()

        by_type(i, do_y, do_z)

    def outs(slot, j):
        return (
            pltpu.make_async_copy(st_d.at[slot], gwd_h.at[:, feat(j)], o_sem.at[0, slot]),
            pltpu.make_async_copy(st_g.at[slot], gwg_h.at[feat(j)], o_sem.at[1, slot]),
            pltpu.make_async_copy(st_u.at[slot], gwu_h.at[feat(j)], o_sem.at[2, slot]),
        )

    def wgrad(j):
        slot = j % 2

        @pl.when(j >= 2)
        def _():
            for copy in outs(slot, j - 2):
                copy.wait()

        st_d[slot] = dot(sh[...], rows[:, :, :, :, feat(j)].reshape(SLOTS, CH), 0, 0).astype(BF)
        xin = inputs[:, :, :, feat(j)].reshape(SLOTS, CH)
        both = dot(xin, dgu[...], 0, 0)
        st_g[slot] = both[:, :FD].astype(BF)
        st_u[slot] = both[:, FD:].astype(BF)
        for copy in outs(slot, j):
            copy.start()

    def send_part(o):
        to = (me + o) % NDEV
        send_to(gpsend.at[to], gprecv.at[me], gp_send, gp_recv, to)

    loop(0, NK, lambda i: pass_on(0, i), lambda i: second(1, i))
    weights[2].wait()
    loop(0, NK, lambda i: settle(0, i))
    loop(0, SIDE, lambda n: pre(0, n))
    to_sibling(0, 0)
    loop(0, NK, lambda i: combine(0, i), lambda i: pass_on(1, i))
    loop(0, NK, lambda i: settle(1, i))
    loop(0, SIDE, lambda n: pre(1, n))
    to_sibling(1, 0)
    loop(0, NK, lambda i: combine(1, i), lambda i: relay(0, i))
    loop(1, NDEV, send_part)
    pltpu.make_async_copy(gpsend.at[me], gprecv.at[me], gp_recv).start()
    loop(
        0, NK, lambda i: wgrad(2 * i), lambda i: relay(1, i), lambda i: wgrad(2 * i + 1)
    )
    for j in (2 * NK - 2, 2 * NK - 1):
        for copy in outs(j % 2, j):
            copy.wait()

    def final(h, i):
        k = chunk(i)
        t = h * NK + k

        def hand(got):
            @pl.when(core == h)
            def _():
                gout[core * NK + k] = got

            @pl.when(core != h)
            def _():
                gsib[k] = got
                send_to(gsib.at[k], gout.at[core * NK + k], gi_send, gi_recv.at[k], sib)

        def do_y(ky):
            wait_bytes(ytok.at[h, ky], c_recv.at[t])
            hand(sum(ytok[h, ky, n].astype(F32) for n in range(SIDE)).astype(BF))

        def do_z(kz):
            wait_bytes(backz.at[h, kz], c_recv.at[t])
            mat = backz[h, kz].reshape(EXPERTS * CAP, CH)
            hand(dot(gmat[h], mat, 1, 0).astype(BF))

        by_type(i, do_y, do_z)

    for h in range(2):

        def finals(k, _):
            final(h, k)
            return 0

        lax.fori_loop(0, NK, finals, 0)

    def put(j):
        return pltpu.make_async_copy(
            gout.at[j], gi_h.at[:, pl.ds(pl.multiple_of(j * CH, CH), CH)], go_sem.at[j]
        )

    def write(k, _):
        put(core * NK + k).start()
        return 0

    lax.fori_loop(0, NK, write, 0)

    wait_bytes(gprecv, gp_recv)
    acc0 = jnp.zeros((TOK, TOK), F32)
    acc1 = jnp.zeros((TOK, TOK), F32)
    for e in range(EXPERTS):
        total = (
            gprecv[4 * e][0:1] + gprecv[4 * e + 1][0:1]
            + gprecv[4 * e + 2][0:1] + gprecv[4 * e + 3][0:1]
        )
        at = lane + e * CAP
        inside = lane < CAP
        acc0 = acc0 + jnp.where((at == tgt[0]) & inside, total, 0.0)
        acc1 = acc1 + jnp.where((at == tgt[1]) & inside, total, 0.0)
    for n, acc in enumerate((acc0, acc1)):
        part = jnp.sum(acc, axis=1, keepdims=True)
        gg_o[n : n + 1, :] = jnp.sum(jnp.where(same, part, 0.0), axis=0, keepdims=True)

    def write_sib(k, _):
        wait_bytes(gout.at[other * NK + k], gi_recv.at[k])
        put(other * NK + k).start()
        return 0

    lax.fori_loop(0, NK, write_sib, 0)

    wait_bytes(xbuf, x_send)
    wait_bytes(trows.at[pl.ds(0, 7)], t_send)
    wait_bytes(grecv.at[pl.ds(0, NDEV - 1)], g_send)
    wait_bytes(gprecv.at[pl.ds(0, NDEV - 1)], gp_send)
    wait_bytes(gsib, gi_send)

    def drain(t, _):
        wait_bytes(comb.at[0, 0, pl.ds(0, SIDE - 1)], q_send.at[t])
        wait_bytes(comb.at[0, 0], s_send.at[t])

        @pl.when(t % NK >= NZ)
        def _():
            wait_bytes(comb.at[0, 0, pl.ds(0, SIDE - 1)], d_send.at[t])
            wait_bytes(ybuf.at[0, 0, pl.ds(0, SIDE - 1)], f_send.at[t])
            wait_bytes(ybuf.at[0, 0, pl.ds(0, SIDE - 1)], c_send.at[t])

        @pl.when(t % NK < NZ)
        def _():
            wait_bytes(zbuf.at[0, 0, pl.ds(0, SIDE - 1)], f_send.at[t])
            wait_bytes(zbuf.at[0, 0, pl.ds(0, SIDE - 1)], c_send.at[t])

        put(t).wait()
        return 0

    lax.fori_loop(0, 2 * NK, drain, 0)
    for slot in range(2):
        wait_bytes(psend.at[slot], p_send.at[slot])


def emit(*refs):
    count = (len(refs) - 1) // 3
    srcs, dsts, bufs, sem = refs[:count], refs[count : 2 * count], refs[2 * count : -1], refs[-1]
    loads, stores = [], []
    n = 0
    for src, dst, buf in zip(srcs, dsts, bufs):
        size = src.shape[0]
        pieces = 4 if size >= 64 else 1
        for p in range(pieces):
            at = pl.ds(p * (size // pieces), size // pieces)
            loads.append(pltpu.make_async_copy(src.at[at], buf.at[at], sem.at[0, n]))
            stores.append(pltpu.make_async_copy(buf.at[at], dst.at[at], sem.at[1, n]))
            n += 1
    for load in loads:
        load.start()
    for load, store in zip(loads, stores):
        load.wait()
        store.start()
    for store in stores:
        store.wait()


def local(nsec, upstream, routes, gates, w_gate, w_up, w_down, stash_q, stash_scale):
    hbm = pl.BlockSpec(memory_space=pl.ANY)
    vmem = pl.BlockSpec(memory_space=pltpu.VMEM)
    dma = pltpu.SemaphoreType.DMA
    v = pltpu.VMEM
    both = 2 * NK
    scratch = [
        v((2, TOK), jnp.int32), v((2, TOK), F32),
        v((2, SIDE, SIDE, CAP, D), BF),
        v((2, NCHIP, CAP, D), BF),
        v((D, 2 * FD), BF), v((FD, D), BF),
        v((SLOTS, FD), F32), v((SLOTS, FD), F32), v((SLOTS, FD), F32),
        v((SLOTS, FD), BF), v((SLOTS, 2 * FD), BF),
        v((NZ, 2, SIDE, 2, CAP, CH), BF), v((NZ, 2, SIDE, 2, CAP, CH), BF),
        v((NY, 2, SIDE, TOK, CH), BF), v((NY, 2, SIDE, SIDE, CAP, CH), BF),
        v((NK, 2, TOK, CH), BF),
        v((2, NK, SIDE, SIDE, CAP, CH), BF),
        v((2, SIDE, SIDE, CAP, CH), BF),
        v((2, NZ, SIDE, SIDE, CAP, CH), BF), v((2, NZ, SIDE, 2, CAP, CH), BF),
        v((2, NY, SIDE, SIDE, CAP, CH), BF), v((2, NY, SIDE, TOK, CH), BF),
        v((both, TOK, CH), BF), v((NK, TOK, CH), BF),
        v((D // 128, 1, SLOTS), F32), v((SLOTS, 32), F32),
        v((2, TOK, EXPERTS * CAP), BF), v((2, EXPERTS * CAP, TOK), BF),
        v((2, SIDE, TOK, SIDE * CAP), BF), v((2, SIDE, SIDE * CAP, TOK), BF),
        v((2, TOK, TOK), jnp.int32),
        v((8, TOK), F32), v((8, 8, TOK), F32),
        v((EXPERTS, 8, TOK), F32), v((NDEV, 8, TOK), F32),
        v((NDEV, 8, TOK), F32), v((NDEV, 8, TOK), F32),
        v((2, FD, CH), BF), v((2, CH, FD), BF), v((2, CH, FD), BF),
        dma, dma((both,)), dma((both,)), dma((both,)), dma((both,)), dma((both,)),
        dma((both,)), dma((both,)), dma((2,)), dma((both,)), dma((both,)), dma((both,)),
        dma((both,)), dma((both,)), dma, dma, dma, dma, dma, dma,
        dma, dma((NK,)), dma((3,)), dma((NFR,)), dma, dma((3, 2)), dma((both,)),
        dma((2,)),
    ]
    shapes = (
        jax.ShapeDtypeStruct((TOK, D), BF),
        jax.ShapeDtypeStruct((2, TOK), F32),
        jax.ShapeDtypeStruct((D, FD), BF),
        jax.ShapeDtypeStruct((D, FD), BF),
        jax.ShapeDtypeStruct((FD, D), BF),
    )
    out = pl.pallas_call(
        functools.partial(kernel, nsec),
        out_shape=shapes,
        in_specs=[hbm] * 8,
        out_specs=(hbm, vmem, hbm, hbm, hbm),
        scratch_shapes=scratch,
        compiler_params=pltpu.CompilerParams(
            collective_id=0, has_side_effects=True, vmem_limit_bytes=67_043_328
        ),
    )(
        routes[0].T, gates[0].T, upstream[0], w_gate[0], w_up[0], w_down[0],
        stash_q.reshape(NCHIP, 2, CAP, D), jnp.transpose(stash_scale, (2, 0, 1)),
    )
    out = pl.pallas_call(
        emit,
        out_shape=shapes,
        in_specs=[hbm] * 5,
        out_specs=(hbm,) * 5,
        scratch_shapes=[v(o.shape, o.dtype) for o in shapes] + [dma((2, 20))],
        compiler_params=pltpu.CompilerParams(vmem_limit_bytes=64_000_000),
    )(*out)
    gi, gg, gwg, gwu, gwd = out
    return gi[None], gg.T[None], gwg[None], gwu[None], gwd[None]


def solution(mesh):
    three = P("section", "expert", None)
    cols = P("section", None, "expert")
    return jax.shard_map(
        functools.partial(local, mesh.shape["section"]),
        mesh=mesh,
        in_specs=(three, three, three, cols, cols, three, three, three),
        out_specs=(three, three, cols, cols, three),
        check_vma=False,
    )
```

```python
import functools

import jax
import jax.numpy as jnp
from jax import lax
from jax.experimental import pallas as pl
from jax.experimental.pallas import tpu as pltpu
from jax.sharding import PartitionSpec as P

EXPERTS = 8
CAP = 48
NCHIP = 16
NDEV = 32
CH = 256
D = 3584
HALF = D // 2
NK = HALF // CH
NZ = 3
NY = NK - NZ
SIDE = 4
SLOTS = NDEV * CAP
FD = 256
TOK = 128
NFR = 8
HSLOTS = SLOTS // 2
PART = HSLOTS // 2
MESH = pl.DeviceIdType.MESH
BF = jnp.bfloat16
F32 = jnp.float32


def dot(a, b, ca, cb):
    return lax.dot_general(a, b, (((ca,), (cb,)), ((), ())), preferred_element_type=F32)


def wait_bytes(ref, sem):
    pltpu.make_async_copy(ref, ref, sem).wait()


def kernel(
    nsec,
    routes_h, gates_h, up_h, wg_h, wu_h, wd_h, sq_h, ss_h,
    gi_h, gg_o, gwg_h, gwu_h, gwd_h,
    routes, gates, up, rows, inputs, wgu, wd, ga, gb, hid, sh, dgu,
    zsend, zbuf, ybuf, ysend, xbuf, comb, psend, cbuf, backz, ybk, ytok, gout, gsib,
    scale, scale_t, gmat, gmat_t, gy, gy_t, tgt, trow, trows,
    gsend, grecv, gpsend, gprecv, st_d, st_g, st_u,
    x_send, x_recv, f_send, f_recv, d_send, d_recv, s_send, s_recv, p_send, p_recv,
    q_send, q_recv, c_send, c_recv, t_send, t_recv, g_send, g_recv, gp_send, gp_recv,
    gi_send, gi_recv, w_sem, sq_sem, ss_sem, o_sem, go_sem, l_sem,
):
    sec = lax.axis_index("section")
    me = lax.axis_index("expert")
    chip = me // 2
    core = me % 2
    sib = me + 1 - 2 * core
    other = 1 - core
    down = (sec + nsec - 1) % nsec
    upper = (sec + 1) % nsec
    z = chip // SIDE
    y = chip % SIDE
    pair = y // 2

    def chunk(i):
        return i // 2 + NZ * (1 - i % 2)

    def send_to(src, dst, ssem, rsem, dev):
        pltpu.make_async_remote_copy(
            src_ref=src, dst_ref=dst, send_sem=ssem, recv_sem=rsem,
            device_id=(sec, dev), device_id_type=MESH,
        ).start()

    def at_z(zz):
        return (zz * SIDE + y) * 2 + core

    def at_y(yy):
        return (z * SIDE + yy) * 2 + core

    def others(body):
        def step(o, _):
            body(o)
            return 0

        lax.fori_loop(1, SIDE, step, 0)

    def feat(j):
        return pl.ds(pl.multiple_of(j * CH, CH), CH)

    def block(h, j):
        return rows.at[h, :, :, :, feat(j)]

    def loop(lo, hi, *steps):
        def body(i, _):
            for step in steps:
                step(i)
            return 0

        lax.fori_loop(lo, hi, body, 0)

    def by_type(i, do_y, do_z):
        if isinstance(i, int):
            (do_z if i % 2 else do_y)(i // 2)
            return

        @pl.when(i % 2 == 0)
        def _():
            do_y(i // 2)

        @pl.when(i % 2 == 1)
        def _():
            do_z(i // 2)

    bar = pltpu.get_barrier_semaphore()

    def greet(o, _):
        pl.semaphore_signal(
            bar, inc=1, device_id=(sec, (me + o) % NDEV), device_id_type=MESH
        )
        return 0

    lax.fori_loop(1, NDEV, greet, 0)
    for sx in (down, upper):
        for cc in range(2):
            pl.semaphore_signal(
                bar, inc=1, device_id=(sx, chip * 2 + cc), device_id_type=MESH
            )

    small = (
        pltpu.make_async_copy(routes_h, routes, l_sem.at[0]),
        pltpu.make_async_copy(gates_h, gates, l_sem.at[1]),
        pltpu.make_async_copy(up_h, up, l_sem.at[2]),
    )
    for copy in small:
        copy.start()
    pltpu.make_async_copy(ss_h, scale, ss_sem).start()

    def stash(f):
        return pltpu.make_async_copy(
            sq_h.at[pl.ds((f % 4) * 4, 4), f // 4],
            inputs.at[f // 4, pl.ds((f % 4) * 4, 4)],
            sq_sem.at[f],
        )

    for f in range(NFR):
        stash(f).start()
    weights = (
        pltpu.make_async_copy(wg_h, wgu.at[:, pl.ds(0, FD)], w_sem.at[0]),
        pltpu.make_async_copy(wu_h, wgu.at[:, pl.ds(FD, FD)], w_sem.at[1]),
        pltpu.make_async_copy(wd_h, wd, w_sem.at[2]),
    )
    for copy in weights:
        copy.start()

    small[0].wait()
    small[1].wait()

    lane = lax.broadcasted_iota(jnp.int32, (TOK, TOK), 1)
    sub = lax.broadcasted_iota(jnp.int32, (TOK, TOK), 0)
    same = lane == sub

    def column(row):
        return jnp.sum(jnp.where(same, row, 0), axis=1, keepdims=True)

    r0 = column(routes[0:1, :])
    r1 = column(routes[1:2, :])
    w0 = column(gates[0:1, :])
    w1 = column(gates[1:2, :])
    o0 = (lane == r0).astype(F32)
    o1 = (lane == r1).astype(F32)
    lower = (lane < sub).astype(BF)
    before = dot(lower, (o0 + o1).astype(BF), 1, 0)
    t0 = r0 * CAP + jnp.sum(before * o0, axis=1, keepdims=True).astype(jnp.int32)
    t1 = r1 * CAP + jnp.sum(before * o1, axis=1, keepdims=True).astype(jnp.int32)
    tgt[0] = jnp.broadcast_to(t0, (TOK, TOK))
    tgt[1] = jnp.broadcast_to(t1, (TOK, TOK))
    trow[...] = jnp.zeros_like(trow)
    for n, t in enumerate((t0, t1)):
        line = jnp.sum(jnp.where(same, t, 0), axis=0, keepdims=True)
        trow[n : n + 1, :] = line.astype(F32)
    for e in range(EXPERTS):
        at = lane + e * CAP
        inside = lane < CAP
        hit = jnp.where((at == t0) & inside, w0, 0.0) + jnp.where((at == t1) & inside, w1, 0.0)
        gsend[e] = jnp.broadcast_to(jnp.sum(hit, axis=0, keepdims=True), (8, TOK))

    small[2].wait()
    pl.semaphore_wait(bar, NDEV - 1 + 4)

    def xs(i):
        k = chunk(i)
        for cc in range(2):
            pltpu.make_async_remote_copy(
                src_ref=up.at[:, pl.ds(pl.multiple_of(cc * HALF + k * CH, CH), CH)],
                dst_ref=xbuf.at[k, core],
                send_sem=x_send,
                recv_sem=x_recv.at[core * NK + k],
                device_id=(down, chip * 2 + cc),
                device_id_type=MESH,
            ).start()

    @pl.when(core == 0)
    def _():
        loop(0, NK, xs)

    spot = me % 8

    def send_rows(o, _):
        to = z * 8 + (spot + o) % 8
        send_to(trow, trows.at[spot], t_send, t_recv, to)
        return 0

    lax.fori_loop(1, 8, send_rows, 0)
    pltpu.make_async_copy(trow, trows.at[spot], t_recv).start()
    def sendg(o, _):
        to = (me + o) % NDEV
        pltpu.make_async_remote_copy(
            src_ref=gsend.at[to // 4], dst_ref=grecv.at[me], send_sem=g_send,
            recv_sem=g_recv, device_id=(sec, to), device_id_type=MESH,
        ).start()
        return 0

    lax.fori_loop(1, NDEV, sendg, 0)
    pltpu.make_async_copy(gsend.at[me // 4], grecv.at[me], g_recv).start()

    def arrived(h, i):
        k = chunk(i)
        wait_bytes(xbuf.at[k, h], x_recv.at[h * NK + k])

    def first_y(h, ky):
        src = xbuf.at[NZ + ky, h]
        dst = ybuf.at[ky, h, y]
        t = h * NK + NZ + ky
        others(lambda o: send_to(src, dst, f_send.at[t], f_recv.at[t], at_y((y + o) % SIDE)))
        pltpu.make_async_copy(src, dst, f_recv.at[t]).start()

    def first_z(h, kz):
        packed = dot(gmat_t[h], xbuf[kz, h], 1, 0).astype(BF)
        zsend[kz, h] = packed.reshape(SIDE, 2, CAP, CH)
        dst = zbuf.at[kz, h, z]
        t = h * NK + kz

        def out(o):
            to = (z + o) % SIDE
            send_to(zsend.at[kz, h, to], dst, f_send.at[t], f_recv.at[t], at_z(to))

        others(out)
        pltpu.make_async_copy(zsend.at[kz, h, z], dst, f_recv.at[t]).start()

    def first(h, i):
        arrived(h, i)
        by_type(i, functools.partial(first_y, h), functools.partial(first_z, h))

    first(0, 0)

    wait_bytes(trows, t_recv)

    def hits(t, axis, size, positions):
        shape = (size, TOK) if axis == 0 else (TOK, size)
        at = positions(lax.broadcasted_iota(jnp.int32, shape, axis))
        lines = [t[n : n + 1].astype(jnp.int32) for n in range(2)]
        if axis == 1:
            lines = [column(line) for line in lines]
        return ((at == lines[0]) | (at == lines[1])).astype(F32).astype(BF)

    def all_slots(at):
        return at

    def pair_slots(at):
        step = sum((at >= n * CAP).astype(jnp.int32) for n in range(1, SIDE))
        return at + (step + pair) * CAP

    for b in range(2):
        gmat_t[b] = hits(trows[y * 2 + b], 0, EXPERTS * CAP, all_slots)
        for n in range(SIDE):
            gy_t[b, n] = hits(trows[n * 2 + b], 0, SIDE * CAP, pair_slots)


    def second(h, i):
        k = chunk(i)
        t = h * NK + k
        j = core * NK + k

        def do_y(ky):
            wait_bytes(ybuf.at[ky, h], f_recv.at[t])
            for n in range(SIDE):
                packed = dot(gy_t[h, n], ybuf[ky, h, n], 1, 0).astype(BF)
                ysend[ky, h, :, n] = packed.reshape(SIDE, CAP, CH)
            dst = rows.at[h, z, :, :, feat(j)]

            def out(o):
                to = (z + o) % SIDE
                send_to(ysend.at[ky, h, to], dst, d_send.at[t], d_recv.at[t], at_z(to))

            others(out)
            pltpu.make_async_copy(ysend.at[ky, h, z], dst, d_recv.at[t]).start()

        def do_z(kz):
            wait_bytes(zbuf.at[kz, h], f_recv.at[t])
            dst = rows.at[h, :, y, :, feat(j)]

            def out(o):
                to = (y + o) % SIDE
                send_to(
                    zbuf.at[kz, h, :, to // 2], dst, d_send.at[t], d_recv.at[t], at_y(to)
                )

            others(out)
            pltpu.make_async_copy(zbuf.at[kz, h, :, pair], dst, d_recv.at[t]).start()

        by_type(i, do_y, do_z)

    def forward(f):
        h = f // 4
        c4 = (f % 4) * 4
        stash(f).wait()

        def dequant(q, _):
            chp = c4 + q
            sc = scale_t[pl.ds(pl.multiple_of((chp * 2 + h) * CAP, CAP), CAP), :]
            for n in range(D // 128):
                cols = slice(n * 128, (n + 1) * 128)
                v = inputs[h, chp, :, cols].astype(F32) * sc[:, n : n + 1]
                inputs[h, chp, :, cols] = v.astype(BF)
            return 0

        lax.fori_loop(0, 4, dequant, 0)
        at = pl.ds(pl.multiple_of(f * 4 * CAP, 4 * CAP), 4 * CAP)
        both = dot(inputs[h, pl.ds(c4, 4)].reshape(4 * CAP, D), wgu[...], 1, 0)
        ga[at] = both[:, :FD]
        gb[at] = both[:, FD:]

    loop(1, 3, lambda i: first(0, i))
    second(0, 0)
    first(0, 3)

    @pl.when(core == 1)
    def _():
        loop(0, NK, xs)

    first(0, 4)
    second(0, 1)

    pltpu.make_async_copy(ss_h, scale, ss_sem).wait()
    for q in range(4):
        for m in range(3):
            at = slice(q * 384 + m * 128, q * 384 + (m + 1) * 128)
            lines = [scale[n, :, at] for n in range(D // 128)]
            lines.append(jnp.zeros((4, 128), F32))
            scale_t[at, :] = jnp.concatenate(lines, axis=0).T

    for b in range(2):
        gmat[b] = hits(trows[y * 2 + b], 1, EXPERTS * CAP, all_slots)
        for n in range(SIDE):
            gy[b, n] = hits(trows[n * 2 + b], 1, SIDE * CAP, pair_slots)
    weights[0].wait()
    weights[1].wait()
    first(0, 5)
    forward(0)
    first(0, 6)
    second(0, 2)
    forward(1)
    loop(3, NK, lambda i: second(0, i), lambda i: first(1, i - 3), lambda i: forward(i - 1))
    loop(4, NK, lambda i: first(1, i))
    loop(6, NFR, forward)

    wait_bytes(grecv, g_recv)
    diag = lax.broadcasted_iota(jnp.int32, (CAP, TOK), 0) == lax.broadcasted_iota(
        jnp.int32, (CAP, TOK), 1
    )

    def factors(b, _):
        at = pl.ds(pl.multiple_of(b * CAP, CAP), CAP)
        source = (b % NCHIP) * 2 + b // NCHIP
        w = jnp.sum(jnp.where(diag, grecv[source][0:1], 0.0), axis=1, keepdims=True)
        g = ga[at]
        u = gb[at]
        sigma = jax.nn.sigmoid(g)
        swish = g * sigma
        h = swish * u
        hid[at] = h
        sh[at] = (w * h).astype(BF)
        ga[at] = w * u * sigma * (1.0 + g * (1.0 - sigma))
        gb[at] = w * swish
        return 0

    lax.fori_loop(0, NDEV, factors, 0)

    def pass_on(h, i):
        k = chunk(i)
        t = h * NK + k
        mine = block(h, core * NK + k)
        wait_bytes(mine, d_recv.at[t])
        send_to(mine, mine, s_send.at[t], s_recv.at[t], sib)

    def settle(h, i):
        k = chunk(i)
        wait_bytes(block(h, other * NK + k), s_recv.at[h * NK + k])

    def pre(h, zz):
        at = pl.ds(pl.multiple_of(h * HSLOTS + zz * SIDE * CAP, SIDE * CAP), SIDE * CAP)
        r = dot(rows[h, zz].reshape(SIDE * CAP, D), wd[...], 1, 1)
        dgu[at, 0:FD] = (r * ga[at]).astype(BF)
        dgu[at, FD : 2 * FD] = (r * gb[at]).astype(BF)
        part = jnp.sum(r * hid[at], axis=1, keepdims=True)
        for n in range(SIDE):
            piece = part[n * CAP : (n + 1) * CAP]
            line = jnp.sum(jnp.where(diag, piece, 0.0), axis=0, keepdims=True)
            gpsend[(zz * SIDE + n) * 2 + h] = jnp.broadcast_to(line, (8, TOK))

    def partial_of(h, j, r):
        at = pl.ds(pl.multiple_of(h * HSLOTS + r * PART, PART), PART)
        return dot(dgu[at], wgu[feat(j)], 1, 1)

    def to_sibling(h, i):
        k = chunk(i)
        turn = h * NK + i
        slot = turn % 2

        @pl.when(turn >= 2)
        def _():
            wait_bytes(psend.at[slot], p_send.at[slot])

        def part(r, _):
            psend[slot, pl.ds(r * 2, 2)] = (
                partial_of(h, other * NK + k, r).astype(BF).reshape(2, SIDE, CAP, CH)
            )
            return 0

        lax.fori_loop(0, 2, part, 0)
        send_to(
            psend.at[slot], comb.at[h, k], p_send.at[slot], p_recv.at[h * NK + k], sib
        )

    def combine(h, i):
        k = chunk(i)
        t = h * NK + k

        @pl.when(i + 1 < NK)
        def _():
            to_sibling(h, i + 1)

        wait_bytes(comb.at[h, k], p_recv.at[t])

        def part(r, _):
            got = comb[h, k, pl.ds(r * 2, 2)].reshape(PART, CH).astype(F32)
            comb[h, k, pl.ds(r * 2, 2)] = (
                (partial_of(h, core * NK + k, r) + got).astype(BF).reshape(2, SIDE, CAP, CH)
            )
            return 0

        lax.fori_loop(0, 2, part, 0)

        def do_y(ky):
            dst = ybk.at[h, ky, z]

            def out(o):
                to = (z + o) % SIDE
                send_to(comb.at[h, k, to], dst, q_send.at[t], q_recv.at[t], at_z(to))

            others(out)
            pltpu.make_async_copy(comb.at[h, k, z], dst, q_recv.at[t]).start()

        def do_z(kz):
            dst = cbuf.at[h, kz, y]

            def out(o):
                to = (y + o) % SIDE
                send_to(comb.at[h, k, :, to], dst, q_send.at[t], q_recv.at[t], at_y(to))

            others(out)
            pltpu.make_async_copy(comb.at[h, k, :, y], dst, q_recv.at[t]).start()

        by_type(i, do_y, do_z)

    def relay(h, i):
        t = h * NK + chunk(i)

        def do_y(ky):
            wait_bytes(ybk.at[h, ky], q_recv.at[t])
            for n in range(SIDE):
                mat = ybk[h, ky, :, n].reshape(SIDE * CAP, CH)
                ybuf[ky, h, n] = dot(gy[h, n], mat, 1, 0).astype(BF)
            dst = ytok.at[h, ky, y]

            def out(o):
                to = (y + o) % SIDE
                send_to(ybuf.at[ky, h, to], dst, c_send.at[t], c_recv.at[t], at_y(to))

            others(out)
            pltpu.make_async_copy(ybuf.at[ky, h, y], dst, c_recv.at[t]).start()

        def do_z(kz):
            wait_bytes(cbuf.at[h, kz], q_recv.at[t])
            wait_bytes(comb.at[0, 0, pl.ds(0, SIDE - 1)], d_send.at[t])
            for n in range(2):
                total = cbuf[h, kz, 2 * n].astype(F32) + cbuf[h, kz, 2 * n + 1].astype(F32)
                zbuf[kz, h, :, n] = total.astype(BF)
            dst = backz.at[h, kz, z]

            def out(o):
                to = (z + o) % SIDE
                send_to(zbuf.at[kz, h, to], dst, c_send.at[t], c_recv.at[t], at_z(to))

            others(out)
            pltpu.make_async_copy(zbuf.at[kz, h, z], dst, c_recv.at[t]).start()

        by_type(i, do_y, do_z)

    def outs(slot, j):
        return (
            pltpu.make_async_copy(st_d.at[slot], gwd_h.at[:, feat(j)], o_sem.at[0, slot]),
            pltpu.make_async_copy(st_g.at[slot], gwg_h.at[feat(j)], o_sem.at[1, slot]),
            pltpu.make_async_copy(st_u.at[slot], gwu_h.at[feat(j)], o_sem.at[2, slot]),
        )

    def wgrad(j):
        slot = j % 2

        @pl.when(j >= 2)
        def _():
            for copy in outs(slot, j - 2):
                copy.wait()

        st_d[slot] = dot(sh[...], rows[:, :, :, :, feat(j)].reshape(SLOTS, CH), 0, 0).astype(BF)
        xin = inputs[:, :, :, feat(j)].reshape(SLOTS, CH)
        both = dot(xin, dgu[...], 0, 0)
        st_g[slot] = both[:, :FD].astype(BF)
        st_u[slot] = both[:, FD:].astype(BF)
        for copy in outs(slot, j):
            copy.start()

    def send_part(o):
        to = (me + o) % NDEV
        send_to(gpsend.at[to], gprecv.at[me], gp_send, gp_recv, to)

    loop(0, NK, lambda i: pass_on(0, i), lambda i: second(1, i))
    weights[2].wait()
    loop(0, NK, lambda i: settle(0, i))
    loop(0, SIDE, lambda n: pre(0, n))
    to_sibling(0, 0)
    loop(0, NK, lambda i: combine(0, i), lambda i: pass_on(1, i))
    loop(0, NK, lambda i: settle(1, i))
    loop(0, SIDE, lambda n: pre(1, n))
    to_sibling(1, 0)
    loop(0, NK, lambda i: combine(1, i), lambda i: relay(0, i))
    loop(1, NDEV, send_part)
    pltpu.make_async_copy(gpsend.at[me], gprecv.at[me], gp_recv).start()
    loop(
        0, NK, lambda i: wgrad(2 * i), lambda i: relay(1, i), lambda i: wgrad(2 * i + 1)
    )
    for j in (2 * NK - 2, 2 * NK - 1):
        for copy in outs(j % 2, j):
            copy.wait()

    def final(h, i):
        k = chunk(i)
        t = h * NK + k

        def hand(got):
            @pl.when(core == h)
            def _():
                gout[core * NK + k] = got

            @pl.when(core != h)
            def _():
                gsib[k] = got
                send_to(gsib.at[k], gout.at[core * NK + k], gi_send, gi_recv.at[k], sib)

        def do_y(ky):
            wait_bytes(ytok.at[h, ky], c_recv.at[t])
            hand(sum(ytok[h, ky, n].astype(F32) for n in range(SIDE)).astype(BF))

        def do_z(kz):
            wait_bytes(backz.at[h, kz], c_recv.at[t])
            mat = backz[h, kz].reshape(EXPERTS * CAP, CH)
            hand(dot(gmat[h], mat, 1, 0).astype(BF))

        by_type(i, do_y, do_z)

    for h in range(2):

        def finals(k, _):
            final(h, k)
            return 0

        lax.fori_loop(0, NK, finals, 0)

    def put(j):
        return pltpu.make_async_copy(
            gout.at[j], gi_h.at[:, pl.ds(pl.multiple_of(j * CH, CH), CH)], go_sem.at[j]
        )

    def write(k, _):
        put(core * NK + k).start()
        return 0

    lax.fori_loop(0, NK, write, 0)

    wait_bytes(gprecv, gp_recv)
    acc0 = jnp.zeros((TOK, TOK), F32)
    acc1 = jnp.zeros((TOK, TOK), F32)
    for e in range(EXPERTS):
        total = (
            gprecv[4 * e][0:1] + gprecv[4 * e + 1][0:1]
            + gprecv[4 * e + 2][0:1] + gprecv[4 * e + 3][0:1]
        )
        at = lane + e * CAP
        inside = lane < CAP
        acc0 = acc0 + jnp.where((at == tgt[0]) & inside, total, 0.0)
        acc1 = acc1 + jnp.where((at == tgt[1]) & inside, total, 0.0)
    for n, acc in enumerate((acc0, acc1)):
        part = jnp.sum(acc, axis=1, keepdims=True)
        gg_o[n : n + 1, :] = jnp.sum(jnp.where(same, part, 0.0), axis=0, keepdims=True)

    def write_sib(k, _):
        wait_bytes(gout.at[other * NK + k], gi_recv.at[k])
        put(other * NK + k).start()
        return 0

    lax.fori_loop(0, NK, write_sib, 0)

    wait_bytes(xbuf, x_send)
    wait_bytes(trows.at[pl.ds(0, 7)], t_send)
    wait_bytes(grecv.at[pl.ds(0, NDEV - 1)], g_send)
    wait_bytes(gprecv.at[pl.ds(0, NDEV - 1)], gp_send)
    wait_bytes(gsib, gi_send)

    def drain(t, _):
        wait_bytes(comb.at[0, 0, pl.ds(0, SIDE - 1)], q_send.at[t])
        wait_bytes(comb.at[0, 0], s_send.at[t])

        @pl.when(t % NK >= NZ)
        def _():
            wait_bytes(comb.at[0, 0, pl.ds(0, SIDE - 1)], d_send.at[t])
            wait_bytes(ybuf.at[0, 0, pl.ds(0, SIDE - 1)], f_send.at[t])
            wait_bytes(ybuf.at[0, 0, pl.ds(0, SIDE - 1)], c_send.at[t])

        @pl.when(t % NK < NZ)
        def _():
            wait_bytes(zbuf.at[0, 0, pl.ds(0, SIDE - 1)], f_send.at[t])
            wait_bytes(zbuf.at[0, 0, pl.ds(0, SIDE - 1)], c_send.at[t])

        put(t).wait()
        return 0

    lax.fori_loop(0, 2 * NK, drain, 0)
    for slot in range(2):
        wait_bytes(psend.at[slot], p_send.at[slot])


def emit(*refs):
    count = (len(refs) - 1) // 3
    srcs, dsts, bufs, sem = refs[:count], refs[count : 2 * count], refs[2 * count : -1], refs[-1]
    loads, stores = [], []
    n = 0
    for src, dst, buf in zip(srcs, dsts, bufs):
        size = src.shape[0]
        pieces = 4 if size >= 64 else 1
        for p in range(pieces):
            at = pl.ds(p * (size // pieces), size // pieces)
            loads.append(pltpu.make_async_copy(src.at[at], buf.at[at], sem.at[0, n]))
            stores.append(pltpu.make_async_copy(buf.at[at], dst.at[at], sem.at[1, n]))
            n += 1
    for load in loads:
        load.start()
    for load, store in zip(loads, stores):
        load.wait()
        store.start()
    for store in stores:
        store.wait()


def local(nsec, upstream, routes, gates, w_gate, w_up, w_down, stash_q, stash_scale):
    hbm = pl.BlockSpec(memory_space=pl.ANY)
    vmem = pl.BlockSpec(memory_space=pltpu.VMEM)
    dma = pltpu.SemaphoreType.DMA
    v = pltpu.VMEM
    both = 2 * NK
    scratch = [
        v((2, TOK), jnp.int32), v((2, TOK), F32), v((TOK, D), BF),
        v((2, SIDE, SIDE, CAP, D), BF),
        v((2, NCHIP, CAP, D), BF),
        v((D, 2 * FD), BF), v((FD, D), BF),
        v((SLOTS, FD), F32), v((SLOTS, FD), F32), v((SLOTS, FD), F32),
        v((SLOTS, FD), BF), v((SLOTS, 2 * FD), BF),
        v((NZ, 2, SIDE, 2, CAP, CH), BF), v((NZ, 2, SIDE, 2, CAP, CH), BF),
        v((NY, 2, SIDE, TOK, CH), BF), v((NY, 2, SIDE, SIDE, CAP, CH), BF),
        v((NK, 2, TOK, CH), BF),
        v((2, NK, SIDE, SIDE, CAP, CH), BF),
        v((2, SIDE, SIDE, CAP, CH), BF),
        v((2, NZ, SIDE, SIDE, CAP, CH), BF), v((2, NZ, SIDE, 2, CAP, CH), BF),
        v((2, NY, SIDE, SIDE, CAP, CH), BF), v((2, NY, SIDE, TOK, CH), BF),
        v((both, TOK, CH), BF), v((NK, TOK, CH), BF),
        v((D // 128, 1, SLOTS), F32), v((SLOTS, 32), F32),
        v((2, TOK, EXPERTS * CAP), BF), v((2, EXPERTS * CAP, TOK), BF),
        v((2, SIDE, TOK, SIDE * CAP), BF), v((2, SIDE, SIDE * CAP, TOK), BF),
        v((2, TOK, TOK), jnp.int32),
        v((8, TOK), F32), v((8, 8, TOK), F32),
        v((EXPERTS, 8, TOK), F32), v((NDEV, 8, TOK), F32),
        v((NDEV, 8, TOK), F32), v((NDEV, 8, TOK), F32),
        v((2, FD, CH), BF), v((2, CH, FD), BF), v((2, CH, FD), BF),
        dma, dma((both,)), dma((both,)), dma((both,)), dma((both,)), dma((both,)),
        dma((both,)), dma((both,)), dma((2,)), dma((both,)), dma((both,)), dma((both,)),
        dma((both,)), dma((both,)), dma, dma, dma, dma, dma, dma,
        dma, dma((NK,)), dma((3,)), dma((NFR,)), dma, dma((3, 2)), dma((both,)),
        dma((3,)),
    ]
    shapes = (
        jax.ShapeDtypeStruct((TOK, D), BF),
        jax.ShapeDtypeStruct((2, TOK), F32),
        jax.ShapeDtypeStruct((D, FD), BF),
        jax.ShapeDtypeStruct((D, FD), BF),
        jax.ShapeDtypeStruct((FD, D), BF),
    )
    out = pl.pallas_call(
        functools.partial(kernel, nsec),
        out_shape=shapes,
        in_specs=[hbm] * 8,
        out_specs=(hbm, vmem, hbm, hbm, hbm),
        scratch_shapes=scratch,
        compiler_params=pltpu.CompilerParams(
            collective_id=0, has_side_effects=True, vmem_limit_bytes=67_043_328
        ),
    )(
        routes[0].T, gates[0].T, upstream[0], w_gate[0], w_up[0], w_down[0],
        stash_q.reshape(NCHIP, 2, CAP, D), jnp.transpose(stash_scale, (2, 0, 1)),
    )
    out = pl.pallas_call(
        emit,
        out_shape=shapes,
        in_specs=[hbm] * 5,
        out_specs=(hbm,) * 5,
        scratch_shapes=[v(o.shape, o.dtype) for o in shapes] + [dma((2, 20))],
        compiler_params=pltpu.CompilerParams(vmem_limit_bytes=64_000_000),
    )(*out)
    gi, gg, gwg, gwu, gwd = out
    return gi[None], gg.T[None], gwg[None], gwu[None], gwd[None]


def solution(mesh):
    three = P("section", "expert", None)
    cols = P("section", None, "expert")
    return jax.shard_map(
        functools.partial(local, mesh.shape["section"]),
        mesh=mesh,
        in_specs=(three, three, three, cols, cols, three, three, three),
        out_specs=(three, three, cols, cols, three),
        check_vma=False,
    )
```
